128 devices in a mesh: ta: 4 (over y), ha: 8 (over z_lo, x), wa: 4 (over z_hi, core).
Axes of the slice: x: 4, y: 4, z: 4 (z_hi: 2, z_lo: 2; z = z_hi * 2 + z_lo), core: 2. Of those that a mesh axis runs over, the one named last changes fastest.
Arguments:
- latent: bfloat16 [16, 128, 128, 256], P('ta', 'ha', 'wa'), may hold values from -6 to 6
- kernel: bfloat16 [27, 256, 256], replicated, may hold values from -0.078125 to 0.078125
- bias: float32 [256], replicated, may hold values from -3 to 3
- cotangent: bfloat16 [16, 128, 128, 256], P('ta', 'ha', 'wa'), may hold values from -6 to 6
Outputs:
- activation: bfloat16 [16, 128, 128, 256], P('ta', 'ha', 'wa')
- latent_grad: bfloat16 [16, 128, 128, 256], P('ta', 'ha', 'wa')
- kernel_grad: float32 [27, 256, 256], replicated
- bias_grad: float32 [256], replicated
The draws below stay inside these ranges and needn't reach their ends.
All inputs are finite; a program needn't handle non-finite values.
Results may differ from the reference program's by a relative error of at most 0.0055.
Values may be sent and summed in bfloat16 or wider, within the bound.
No kernel may reach another device: no remote copies, remote signals or barrier semaphores. Data moves between devices by JAX's collectives and lax.ppermute only.
A program may use at most 128 MiB of HBM per device.

```python
import jax
import jax.numpy as jnp
from jax import lax

C = 256
NT = 16
NH = 128
NW = 128


def block_levels(rng, shape, cuts, low, top_value):
    level, own = 1.0, jax.random.fold_in(rng, 6)
    for dim, parts in cuts:
        heights = jnp.exp(jax.random.uniform(jax.random.fold_in(own, dim), (parts,), jnp.float32, low / len(cuts), top_value / len(cuts)))
        level = level * jnp.repeat(heights, shape[dim] // parts).reshape([-1 if axis == dim else 1 for axis in range(len(shape))])
    return level


def noise(own_key, dims, scale, reach, split=(), held_as=jnp.bfloat16):
    drawn = jax.random.normal(own_key, dims, jnp.float32) * scale
    if len(split) > 0:
        drawn = block_levels(own_key, dims, split, -0.22, 0.18) * drawn
    return jnp.clip(drawn, min=-reach, max=reach).astype(held_as)


def setup_inputs(seed: int = 0) -> dict:
    key_of = jax.random.split(jax.random.key(seed), 5)
    latent = noise(key_of[0], (NT, NH, NW, C), 1.0, 6.0, ((0, 4), (1, 8), (2, 4)))
    kernel = noise(key_of[1], (27, C, C), (27 * C) ** -0.5, 0.078125)
    bias = noise(key_of[2], (C,), 0.5, 3.0, (), jnp.float32)
    cotangent = noise(key_of[3], (NT, NH, NW, C), 1.0, 6.0, ((0, 4), (1, 8), (2, 4)))
    return {"latent": latent, "kernel": kernel, "bias": bias, "cotangent": cotangent}


def convolve(padded, kernel, frames, rows, columns):
    width = kernel.shape[1]
    grouped = kernel.reshape(9, 3 * width, kernel.shape[2])
    total = jnp.zeros((frames * rows * columns, kernel.shape[2]), jnp.float32)
    for shift_t in range(3):
        for shift_h in range(3):
            pieces = [padded[shift_t:shift_t + frames, shift_h:shift_h + rows, shift_w:shift_w + columns] for shift_w in range(3)]
            columns_mat = jnp.concatenate(pieces, axis=-1).reshape(-1, 3 * width)
            total = total + jnp.dot(columns_mat, grouped[3 * shift_t + shift_h], preferred_element_type=jnp.float32)
    return total

def kernel_terms(padded, dflat, frames, rows, columns):
    width = padded.shape[-1]
    blocks = []
    for shift_t in range(3):
        for shift_h in range(3):
            pieces = [padded[shift_t:shift_t + frames, shift_h:shift_h + rows, shift_w:shift_w + columns] for shift_w in range(3)]
            columns_mat = jnp.concatenate(pieces, axis=-1).reshape(-1, 3 * width)
            blocks.append(lax.dot_general(columns_mat, dflat, (((0,), (0,)), ((), ())), preferred_element_type=jnp.float32))
    return jnp.stack(blocks).reshape(27, width, dflat.shape[1])

def flipped(kernel):
    width = kernel.shape[1]
    return kernel.reshape(3, 3, 3, width, width)[::-1, ::-1, ::-1].transpose(0, 1, 2, 4, 3).reshape(27, width, width)

def reference(latent, kernel, bias, cotangent):
    frames, rows, columns, width = latent.shape
    padded = jnp.pad(latent, ((2, 0), (1, 1), (1, 1), (0, 0)))
    pre = convolve(padded, kernel, frames, rows, columns) + bias[None, :]
    sig = jax.nn.sigmoid(pre)
    activation = (pre * sig).astype(jnp.bfloat16).reshape(frames, rows, columns, width)
    cot = cotangent.reshape(-1, width).astype(jnp.float32)
    dflat = (cot * sig * (1.0 + pre * (1.0 - sig))).astype(jnp.bfloat16)
    dpadded = jnp.pad(dflat.reshape(frames, rows, columns, width), ((0, 2), (1, 1), (1, 1), (0, 0)))
    latent_grad = convolve(dpadded, flipped(kernel), frames, rows, columns).astype(jnp.bfloat16).reshape(frames, rows, columns, width)
    scale = 1.0 / jnp.sqrt(jnp.float32(frames * rows * columns))
    kernel_grad = kernel_terms(padded, dflat, frames, rows, columns) * scale
    bias_grad = lax.optimization_barrier(jnp.sum(dflat.astype(jnp.float32), axis=0)) * scale
    return (activation, latent_grad, kernel_grad, bias_grad)
```

```python
import functools
import itertools

import jax
import jax.numpy as jnp
import numpy as np
from jax import lax
from jax.experimental import pallas as pl
from jax.experimental.pallas import tpu as pltpu
from jax.sharding import Mesh
from jax.sharding import PartitionSpec as P

AXES = ("ta", "hz", "hx", "wz", "wc")
HA = ("hz", "hx")
WA = ("wz", "wc")
BF = jnp.bfloat16
F32 = jnp.float32
HALF = 14
VMEM = pl.BlockSpec(memory_space=pltpu.VMEM)
MIB = 1 << 20


def number(x, y, z, core):
    return (((y * 2 + z % 2) * 4 + x) * 2 + z // 2) * 2 + core


def cubes(pairs):
    out = []
    for core in (0, 1):
        for px, py, pz in itertools.product(pairs, repeat=3):
            cube = []
            for a, b, c in itertools.product(range(2), repeat=3):
                place = [(p + core) % 4 for p in (px[a], py[b], pz[c])]
                cube.append(number(*place, core))
            out.append(cube)
    return out


NEAR = cubes(((0, 1), (3, 2)))
FAR = cubes(((0, 3), (1, 2)))


def exchange(pieces, groups):
    return lax.all_to_all(pieces, AXES, 0, 0, axis_index_groups=groups)


def shift(block, axis, distance):
    names = axis if isinstance(axis, tuple) else (axis,)
    count = 1
    for name in names:
        count *= lax.axis_size(name)
    route = [(i, i + distance) for i in range(count) if 0 <= i + distance < count]
    return lax.ppermute(block, axis, route)


def halo(field, near_frames, direction):
    frames = field.shape[0]
    remote = shift(near_frames(field), "ta", direction)
    low = shift(field[:, -1:], HA, 1)
    high = shift(field[:, :1], HA, -1)
    last = jnp.concatenate([low[:, :, -1:], field[:, :, -1:], high[:, :, -1:]], axis=1)
    first = jnp.concatenate([low[:, :, :1], field[:, :, :1], high[:, :, :1]], axis=1)
    left = shift(last, WA, 1)
    right = shift(first, WA, -1)
    rows = jnp.stack([near_frames(low), near_frames(high)])
    columns = jnp.stack([near_frames(left), near_frames(right)])
    count = rows.size // rows.shape[-1]
    flat = jnp.concatenate([rows.reshape(count, -1), columns.reshape(-1, rows.shape[-1])])
    flat = shift(flat, "ta", direction)
    rows = flat[:count].reshape(rows.shape)
    columns = flat[count:].reshape(columns.shape)
    return (field, low, high, left, right, remote, rows, columns)


def place(parts, own, far, taps):
    field, low, high, left, right, remote, rows, columns = parts
    _, height, width, depth = field.shape

    def put(at, middle, top, bottom, west, east):
        block = jnp.concatenate([top, middle, bottom], axis=0).astype(F32)
        column = lax.broadcasted_iota(jnp.int32, block.shape, 1)
        taps[1, at] = block.astype(BF)
        moved = pltpu.roll(block, 1, 1)
        taps[0, at] = jnp.where(column == 0, west.astype(F32), moved).astype(BF)
        moved = pltpu.roll(block, width - 1, 1)
        taps[2, at] = jnp.where(column == width - 1, east.astype(F32), moved).astype(BF)

    @pl.loop(0, 4)
    def _(t):
        put(own + t, field[t], low[t], high[t], left[t], right[t])

    @pl.loop(0, 2)
    def _(t):
        put(far + t, remote[t], rows[0, t], rows[1, t], columns[0, t], columns[1, t])


def window(taps, c, frame, b):
    piece = taps[c, frame, pl.ds(b, 16)]
    return piece.reshape(-1, piece.shape[-1])


def forward_kernel(*refs):
    parts, (kernel, bias, cotangent), rest = refs[:8], refs[8:11], refs[11:]
    activation, dpre, dpre_t, taps, send = rest
    place(parts, 2, 0, taps)

    @pl.loop(0, 4)
    def _(t):
        total = jnp.broadcast_to(bias[...], (512, 256))
        for a in range(3):
            pieces = [window(taps, c, t + a, b) for b in range(3) for c in range(3)]
            total = total + jnp.dot(
                jnp.concatenate(pieces, axis=1), kernel[a], preferred_element_type=F32
            )
        sig = jax.nn.sigmoid(total)
        activation[t] = (total * sig).astype(BF).reshape(16, 32, 256)
        cot = cotangent[t].reshape(512, 256).astype(F32)
        slope = cot * sig * (1.0 + total * (1.0 - sig))
        dpre[t] = slope.astype(BF).reshape(16, 32, 256)
        dpre_t[:, pl.ds(pl.multiple_of(t * 512, 512), 512)] = slope.T.astype(BF)

    first = HALF * (1 - lax.axis_index("wc"))

    def emit(j, value):
        send[j] = value.astype(BF)

    weight_terms(taps, dpre_t, first, emit)


def weight_terms(taps, dpre_t, first, emit):
    @pl.loop(0, HALF)
    def _(j):
        k = first + j

        @pl.when(k < 27)
        def _():
            a, b, c = k // 9, (k // 3) % 3, k % 3
            block = taps[c, pl.ds(a, 4), pl.ds(b, 16)].reshape(2048, 256)
            emit(j, jnp.dot(dpre_t[...], block, preferred_element_type=F32))

        @pl.when(k == 27)
        def _():
            total = jnp.sum(dpre_t[...].astype(F32), axis=1, keepdims=True)
            high = total.astype(BF).astype(F32)
            lane = lax.broadcasted_iota(jnp.int32, (256, 256), 1)
            emit(j, jnp.where(lane < 128, high, total - high))


def weight_kernel(taps, dpre_t, received, out):
    def emit(j, value):
        out[j] = (value + received[j].astype(F32)).astype(BF)

    weight_terms(taps, dpre_t, HALF * lax.axis_index("wc"), emit)


def backward_kernel(*refs):
    parts, (turned, latent_grad, taps) = refs[:8], refs[8:]
    place(parts, 0, 4, taps)

    @pl.loop(0, 4)
    def _(t):
        total = jnp.zeros((512, 256), F32)
        for a in range(3):
            pieces = [window(taps, 2 - c, t + 2 - a, 2 - b) for b in range(3) for c in range(3)]
            total = total + jnp.dot(
                jnp.concatenate(pieces, axis=1), turned[a], preferred_element_type=F32
            )
        latent_grad[t] = total.astype(BF).reshape(16, 32, 256)


def turn_kernel(kernel, out):
    @pl.loop(0, 27)
    def _(k):
        out[k] = kernel[k].astype(F32).T.astype(BF)


def finish_kernel(scale, mine, other, kernel_grad, bias_grad):
    step = pl.program_id(0)
    k = jnp.where(step == 0, 27, step - 1)
    core = lax.axis_index("wc")
    row = lax.broadcasted_iota(jnp.int32, (256, 256), 0)
    lane = lax.broadcasted_iota(jnp.int32, (256, 256), 1)
    unit = jnp.where(row == lane, 1.0, 0.0).astype(BF)

    def flip(block):
        turned = lax.dot_general(unit, block, (((1,), (1,)), ((), ())), preferred_element_type=F32)

        @pl.when(step == 0)
        def _():
            bias_grad[...] = (turned[0:1] + turned[128:129]) * scale

        @pl.when(step > 0)
        def _():
            kernel_grad[0] = turned * scale

    owner = k // HALF
    j = k - HALF * owner

    @pl.when(owner == core)
    def _():
        flip(mine[j])

    @pl.when(owner != core)
    def _():
        flip(other[j])


def call(body, outs, scratch=(), vmem=48, flops=0, n_in=0):
    return pl.pallas_call(
        body,
        out_shape=outs,
        in_specs=[VMEM] * n_in,
        out_specs=jax.tree.map(lambda _: VMEM, outs),
        scratch_shapes=list(scratch),
        compiler_params=pltpu.CompilerParams(vmem_limit_bytes=vmem * MIB),
        cost_estimate=pl.CostEstimate(flops=flops, bytes_accessed=8 * MIB, transcendentals=0),
    )


def sum_pieces(pieces, special):
    total = jnp.sum(pieces.astype(F32), axis=0)
    value = total[:, :128] + total[:, 128:]
    high = lax.reduce_precision(value, 8, 7)
    split = jnp.concatenate([high, value - high], axis=1)
    return jnp.where(special, split, total).astype(BF)


def shards(latent, kernel, bias, cotangent):
    frames, rows, columns, width = latent.shape
    cells = frames * rows * columns
    for name in AXES:
        cells *= lax.axis_size(name)
    scale = float(1.0 / np.sqrt(np.float32(cells)))
    conv_flops = 2 * 2048 * 27 * 256 * 256
    block = jax.ShapeDtypeStruct(latent.shape, BF)

    turned = call(
        turn_kernel, jax.ShapeDtypeStruct(kernel.shape, BF), vmem=16, flops=conv_flops // 4, n_in=1
    )(kernel)
    padded = halo(latent, lambda x: x[2:], 1)
    half = jax.ShapeDtypeStruct((HALF, 256, 256), BF)
    activation, dpre, dpre_t, taps, send = call(
        forward_kernel,
        (
            block,
            block,
            jax.ShapeDtypeStruct((256, 2048), BF),
            jax.ShapeDtypeStruct((3, 6, 18, 32, 256), BF),
            half,
        ),
        flops=conv_flops * 3 // 2,
        n_in=11,
    )(*padded, kernel.reshape(3, 2304, 256), bias.reshape(1, 256), cotangent)
    received = lax.ppermute(send, "wc", [(0, 1), (1, 0)])
    terms = call(weight_kernel, half, flops=conv_flops // 2, n_in=3)(taps, dpre_t, received)

    core = lax.axis_index("wc")
    z = 2 * lax.axis_index("wz") + lax.axis_index("hz")
    spot = [(p - core) % 4 for p in (lax.axis_index("hx"), lax.axis_index("ta"), z)]
    near = sum(w * ((p == 1) | (p == 2)) for w, p in zip((4, 2, 1), spot))
    far = sum(w * (p >= 2) for w, p in zip((4, 2, 1), spot))
    first_bias = (HALF - 1) * 256

    pieces = exchange(terms.reshape(8, 448, 256), NEAR)
    row = near * 448 + lax.broadcasted_iota(jnp.int32, (448, 1), 0)
    total = sum_pieces(pieces, (core == 1) & (row >= first_bias))
    pieces = exchange(total.reshape(8, 56, 256), FAR)
    row = near * 448 + far * 56 + lax.broadcasted_iota(jnp.int32, (56, 1), 0)
    total = sum_pieces(pieces, (core == 1) & (row >= first_bias))
    total = exchange(jnp.broadcast_to(total[None], (8, 56, 256)), FAR).reshape(448, 256)
    total = exchange(jnp.broadcast_to(total[None], (8, 448, 256)), NEAR)
    mine = total.reshape(HALF, 256, 256)
    other = lax.ppermute(mine, "wc", [(0, 1), (1, 0)])

    spread = halo(dpre, lambda x: x[:2], -1)
    latent_grad = call(
        backward_kernel,
        block,
        (pltpu.VMEM((3, 6, 18, 32, 256), BF),),
        flops=conv_flops,
        n_in=9,
    )(*spread, turned.reshape(3, 2304, 256))

    whole = pl.BlockSpec((HALF, 256, 256), lambda k: (0, 0, 0))
    kernel_grad, bias_grad = pl.pallas_call(
        functools.partial(finish_kernel, scale),
        grid=(28,),
        out_shape=(
            jax.ShapeDtypeStruct((27, 256, 256), F32),
            jax.ShapeDtypeStruct((1, 256), F32),
        ),
        in_specs=[whole, whole],
        out_specs=(
            pl.BlockSpec((1, 256, 256), lambda k: (jnp.maximum(k - 1, 0), 0, 0)),
            pl.BlockSpec((1, 256), lambda k: (0, 0)),
        ),
        compiler_params=pltpu.CompilerParams(vmem_limit_bytes=24 * MIB),
    )(mine, other)
    return (activation, latent_grad, kernel_grad, bias_grad.reshape(256))


def solution(mesh):
    split = Mesh(np.asarray(mesh.devices).reshape(4, 2, 4, 2, 2), AXES)
    placed = P("ta", HA, WA, None)
    return jax.shard_map(
        shards,
        mesh=split,
        in_specs=(placed, P(), P(), placed),
        out_specs=(placed, placed, P(), P()),
        check_vma=False,
    )
```

```python
import functools
import itertools

import jax
import jax.numpy as jnp
import numpy as np
from jax import lax
from jax.experimental import pallas as pl
from jax.experimental.pallas import tpu as pltpu
from jax.sharding import Mesh
from jax.sharding import PartitionSpec as P

AXES = ("ta", "hz", "hx", "wz", "wc")
HA = ("hz", "hx")
WA = ("wz", "wc")
BF = jnp.bfloat16
F32 = jnp.float32
VMEM = pl.BlockSpec(memory_space=pltpu.VMEM)
MIB = 1 << 20


def number(x, y, z, core):
    return (((y * 2 + z % 2) * 4 + x) * 2 + z // 2) * 2 + core


def cubes(pairs):
    out = []
    for core in (0, 1):
        for px, py, pz in itertools.product(pairs, repeat=3):
            cube = []
            for a, b, c in itertools.product(range(2), repeat=3):
                place = [(p + core) % 4 for p in (px[a], py[b], pz[c])]
                cube.append(number(*place, core))
            out.append(cube)
    return out


NEAR = cubes(((0, 1), (3, 2)))
FAR = cubes(((0, 3), (1, 2)))


def exchange(pieces, groups):
    return lax.all_to_all(pieces, AXES, 0, 0, axis_index_groups=groups)


def shift(block, axis, distance):
    names = axis if isinstance(axis, tuple) else (axis,)
    count = 1
    for name in names:
        count *= lax.axis_size(name)
    route = [(i, i + distance) for i in range(count) if 0 <= i + distance < count]
    return lax.ppermute(block, axis, route)


def halo(field, near_frames, direction):
    frames = field.shape[0]
    remote = shift(near_frames(field), "ta", direction)
    low = shift(field[:, -1:], HA, 1)
    high = shift(field[:, :1], HA, -1)
    last = jnp.concatenate([low[:, :, -1:], field[:, :, -1:], high[:, :, -1:]], axis=1)
    first = jnp.concatenate([low[:, :, :1], field[:, :, :1], high[:, :, :1]], axis=1)
    left = shift(last, WA, 1)
    right = shift(first, WA, -1)
    rows = jnp.stack([near_frames(low), near_frames(high)])
    columns = jnp.stack([near_frames(left), near_frames(right)])
    count = rows.size // rows.shape[-1]
    flat = jnp.concatenate([rows.reshape(count, -1), columns.reshape(-1, rows.shape[-1])])
    flat = shift(flat, "ta", direction)
    rows = flat[:count].reshape(rows.shape)
    columns = flat[count:].reshape(columns.shape)
    return (field, low, high, left, right, remote, rows, columns)


def place(parts, own, far, taps):
    field, low, high, left, right, remote, rows, columns = parts
    _, height, width, depth = field.shape

    def put(at, middle, top, bottom, west, east):
        block = jnp.concatenate([top, middle, bottom], axis=0).astype(F32)
        column = lax.broadcasted_iota(jnp.int32, block.shape, 1)
        taps[1, at] = block.astype(BF)
        moved = pltpu.roll(block, 1, 1)
        taps[0, at] = jnp.where(column == 0, west.astype(F32), moved).astype(BF)
        moved = pltpu.roll(block, width - 1, 1)
        taps[2, at] = jnp.where(column == width - 1, east.astype(F32), moved).astype(BF)

    @pl.loop(0, 4)
    def _(t):
        put(own + t, field[t], low[t], high[t], left[t], right[t])

    @pl.loop(0, 2)
    def _(t):
        put(far + t, remote[t], rows[0, t], rows[1, t], columns[0, t], columns[1, t])


def window(taps, c, frame, b):
    piece = taps[c, frame, pl.ds(b, 16)]
    return piece.reshape(-1, piece.shape[-1])


def weight_terms(taps, slope, half, emit):
    lanes = pl.ds(pl.multiple_of(half * 128, 128), 128)

    @pl.loop(0, 3)
    def _(a):
        pieces = [
            taps[c, pl.ds(a, 4), b : b + 16, :, lanes].reshape(2048, 128)
            for b in range(3)
            for c in range(3)
        ]
        value = lax.dot_general(
            jnp.concatenate(pieces, axis=1),
            slope[...].reshape(2048, 256),
            (((0,), (0,)), ((), ())),
            preferred_element_type=F32,
        )
        emit(pl.ds(9 * a, 9), value.reshape(9, 128, 256))


def bias_rows(value):
    high = value.astype(BF).astype(F32)
    return jnp.concatenate([high, value - high, jnp.zeros((112, 256), F32)], axis=0)


def bias_term(slope):
    total = jnp.sum(slope[...].reshape(2048, 256).astype(F32), axis=0, keepdims=True)
    return jnp.broadcast_to(total, (8, 256))


def forward_kernel(*refs):
    parts, (kernel, bias, cotangent), rest = refs[:8], refs[8:11], refs[11:]
    activation, dpre, taps, send = rest
    place(parts, 2, 0, taps)

    @pl.loop(0, 4)
    def _(t):
        total = jnp.broadcast_to(bias[...], (512, 256))
        for a in range(3):
            pieces = [window(taps, c, t + a, b) for b in range(3) for c in range(3)]
            total = total + jnp.dot(
                jnp.concatenate(pieces, axis=1), kernel[a], preferred_element_type=F32
            )
        sig = jax.nn.sigmoid(total)
        activation[t] = (total * sig).astype(BF).reshape(16, 32, 256)
        cot = cotangent[t].reshape(512, 256).astype(F32)
        slope = cot * sig * (1.0 + total * (1.0 - sig))
        dpre[t] = slope.astype(BF).reshape(16, 32, 256)

    def emit(at, value):
        send[at] = value.astype(BF)

    weight_terms(taps, dpre, 1 - lax.axis_index("wc"), emit)
    send[27] = bias_rows(bias_term(dpre)).astype(BF)


def weight_kernel(taps, dpre, out):
    def emit(at, value):
        out[at] = value

    weight_terms(taps, dpre, lax.axis_index("wc"), emit)
    out[27, 0:8] = bias_term(dpre)


def join_kernel(own, received, out):
    out[0:27] = (own[0:27] + received[0:27].astype(F32)).astype(BF)
    value = own[27, 0:8] + received[27, 0:8].astype(F32) + received[27, 8:16].astype(F32)
    out[27] = bias_rows(value).astype(BF)


def sum_kernel(local, pieces, flag, out):
    total = pieces[0].astype(F32)
    for i in range(1, 8):
        total = total + pieces[i].astype(F32)
    rows = total.shape[0]
    total = total.astype(BF)
    copies = out.shape[0] // rows
    for i in range(copies):
        out[i * rows : (i + 1) * rows] = total

    @pl.when(flag[0] == 1)
    def _():
        value = sum(pieces[i, local : local + 16].astype(F32) for i in range(8))
        value = bias_rows(value[0:8] + value[8:16])[0:16].astype(BF)
        for i in range(copies):
            out[i * rows + local : i * rows + local + 16] = value


def backward_kernel(*refs):
    parts, (turned, latent_grad, taps) = refs[:8], refs[8:]
    place(parts, 0, 4, taps)

    @pl.loop(0, 4)
    def _(t):
        total = jnp.zeros((512, 256), F32)
        for a in range(3):
            pieces = [window(taps, 2 - c, t + 2 - a, 2 - b) for b in range(3) for c in range(3)]
            total = total + jnp.dot(
                jnp.concatenate(pieces, axis=1), turned[a], preferred_element_type=F32
            )
        latent_grad[t] = total.astype(BF).reshape(16, 32, 256)


def turn_kernel(kernel, out):
    @pl.loop(0, 27)
    def _(k):
        out[k] = kernel[k].astype(F32).T.astype(BF)


def finish_kernel(scale, mine, other, bias_mine, kernel_grad, bias_grad):
    core = lax.axis_index("wc")
    kernel_grad[:, pl.ds(pl.multiple_of(core * 128, 128), 128)] = mine[...].astype(F32) * scale
    at = pl.ds(pl.multiple_of(128 - core * 128, 128), 128)
    kernel_grad[:, at] = other[...].astype(F32) * scale
    bias_grad[...] = (bias_mine[0, 0:1].astype(F32) + bias_mine[0, 8:9].astype(F32)) * scale


def call(body, outs, scratch=(), vmem=24, flops=0, specs=(), n_in=0):
    return pl.pallas_call(
        body,
        out_shape=outs,
        in_specs=list(specs) or [VMEM] * n_in,
        out_specs=jax.tree.map(lambda _: VMEM, outs),
        scratch_shapes=list(scratch),
        compiler_params=pltpu.CompilerParams(vmem_limit_bytes=vmem * MIB),
        cost_estimate=pl.CostEstimate(flops=flops, bytes_accessed=8 * MIB, transcendentals=0),
    )


def sum_pieces(pieces, local, special, copies):
    rows = pieces.shape[1]
    return call(
        functools.partial(sum_kernel, local),
        jax.ShapeDtypeStruct((copies * rows, 256), BF),
        vmem=12,
        specs=(VMEM, pl.BlockSpec(memory_space=pltpu.SMEM)),
    )(pieces, special.astype(jnp.int32).reshape(1))


def shards(latent, kernel, bias, cotangent):
    frames, rows, columns, width = latent.shape
    cells = frames * rows * columns
    for name in AXES:
        cells *= lax.axis_size(name)
    scale = float(1.0 / np.sqrt(np.float32(cells)))
    conv_flops = 2 * 2048 * 27 * 256 * 256
    block = jax.ShapeDtypeStruct(latent.shape, BF)
    half = (28, 128, 256)

    turned = call(
        turn_kernel, jax.ShapeDtypeStruct(kernel.shape, BF), vmem=16, flops=conv_flops // 4, n_in=1
    )(kernel)
    padded = halo(latent, lambda x: x[2:], 1)
    padded, turned = lax.optimization_barrier((padded, turned))
    activation, dpre, taps, send = call(
        forward_kernel,
        (
            block,
            block,
            jax.ShapeDtypeStruct((3, 6, 18, 32, 256), BF),
            jax.ShapeDtypeStruct(half, BF),
        ),
        vmem=28,
        flops=conv_flops * 3 // 2,
        n_in=11,
    )(*padded, kernel.reshape(3, 2304, 256), bias.reshape(1, 256), cotangent)
    received = lax.ppermute(send, "wc", [(0, 1), (1, 0)])
    own = call(
        weight_kernel, jax.ShapeDtypeStruct(half, F32), flops=conv_flops // 2, n_in=2
    )(taps, dpre)
    terms = call(join_kernel, jax.ShapeDtypeStruct(half, BF), vmem=16, n_in=2)(own, received)

    core = lax.axis_index("wc")
    z = 2 * lax.axis_index("wz") + lax.axis_index("hz")
    spot = [(p - core) % 4 for p in (lax.axis_index("hx"), lax.axis_index("ta"), z)]
    near = sum(w * ((p == 1) | (p == 2)) for w, p in zip((4, 2, 1), spot))
    far = sum(w * (p >= 2) for w, p in zip((4, 2, 1), spot))
    pieces = exchange(terms.reshape(8, 448, 256), NEAR)
    spread = halo(dpre, lambda x: x[:2], -1)
    total = sum_pieces(pieces, 320, near == 7, 1)
    pieces = exchange(total.reshape(8, 56, 256), FAR)
    total = sum_pieces(pieces, 40, (near == 7) & (far == 5), 8)
    total, spread = lax.optimization_barrier((total, spread))
    total = exchange(total.reshape(8, 56, 256), FAR).reshape(448, 256)
    latent_grad = call(
        backward_kernel,
        block,
        (pltpu.VMEM((3, 6, 18, 32, 256), BF),),
        flops=conv_flops,
        n_in=9,
    )(*spread, turned.reshape(3, 2304, 256))
    total = exchange(jnp.broadcast_to(total[None], (8, 448, 256)), NEAR)
    total, latent_grad = lax.optimization_barrier((total, latent_grad))
    mine = total.reshape(half)
    other = lax.ppermute(mine, "wc", [(0, 1), (1, 0)])

    part = pl.BlockSpec((3, 128, 256), lambda k: (k, 0, 0))
    kernel_grad, bias_grad = pl.pallas_call(
        functools.partial(finish_kernel, scale),
        grid=(9,),
        out_shape=(
            jax.ShapeDtypeStruct((27, 256, 256), F32),
            jax.ShapeDtypeStruct((1, 256), F32),
        ),
        in_specs=[part, part, pl.BlockSpec((1, 128, 256), lambda k: (27, 0, 0))],
        out_specs=(
            pl.BlockSpec((3, 256, 256), lambda k: (k, 0, 0)),
            pl.BlockSpec((1, 256), lambda k: (0, 0)),
        ),
        compiler_params=pltpu.CompilerParams(vmem_limit_bytes=12 * MIB),
    )(mine, other, mine)
    return (activation, latent_grad, kernel_grad, bias_grad.reshape(256))


def solution(mesh):
    split = Mesh(np.asarray(mesh.devices).reshape(4, 2, 4, 2, 2), AXES)
    placed = P("ta", HA, WA, None)
    return jax.shard_map(
        shards,
        mesh=split,
        in_specs=(placed, P(), P(), placed),
        out_specs=(placed, placed, P(), P()),
        check_vma=False,
    )
```

```python
import functools
import itertools

import jax
import jax.numpy as jnp
import numpy as np
from jax import lax
from jax.experimental import pallas as pl
from jax.experimental.pallas import tpu as pltpu
from jax.sharding import Mesh
from jax.sharding import PartitionSpec as P

AXES = ("ta", "hz", "hx", "wz", "wc")
HA = ("hz", "hx")
WA = ("wz", "wc")
BF = jnp.bfloat16
F32 = jnp.float32
VMEM = pl.BlockSpec(memory_space=pltpu.VMEM)
ANY = pl.BlockSpec(memory_space=pl.ANY)
MIB = 1 << 20


def number(x, y, z, core):
    return (((y * 2 + z % 2) * 4 + x) * 2 + z // 2) * 2 + core


def cubes(pairs):
    out = []
    for core in (0, 1):
        for px, py, pz in itertools.product(pairs, repeat=3):
            cube = []
            for a, b, c in itertools.product(range(2), repeat=3):
                place = [(p + core) % 4 for p in (px[a], py[b], pz[c])]
                cube.append(number(*place, core))
            out.append(cube)
    return out


NEAR = cubes(((0, 1), (3, 2)))
FAR = cubes(((0, 3), (1, 2)))


def exchange(pieces, groups):
    return lax.all_to_all(pieces, AXES, 0, 0, axis_index_groups=groups)


def shift(block, axis, distance):
    names = axis if isinstance(axis, tuple) else (axis,)
    count = 1
    for name in names:
        count *= lax.axis_size(name)
    route = [(i, i + distance) for i in range(count) if 0 <= i + distance < count]
    return lax.ppermute(block, axis, route)


def transfers(sems, *pairs):
    copies = [pltpu.make_async_copy(s, d, sems.at[i]) for i, (s, d) in enumerate(pairs)]
    for copy in copies:
        copy.start()
    return copies


def one_hot(shape, hit):
    row = lax.broadcasted_iota(jnp.int32, shape, 0)
    lane = lax.broadcasted_iota(jnp.int32, shape, 1)
    return jnp.where(hit(row, lane), 1.0, 0.0).astype(BF)


def edge_rows_kernel(*refs):
    sems = refs[-1]
    field, outs = refs[0], refs[1:-1]
    pairs = [
        (field.at[:, pl.ds(0, 1)], outs[0]),
        (field.at[:, pl.ds(15, 1)], outs[1]),
        (field.at[pl.ds(2, 2)], outs[2]),
    ]
    for copy in transfers(sems, *pairs):
        copy.wait()


def more_rows_kernel(field, remote, top, bottom, sems):
    pairs = []
    for out, row in ((top, 0), (bottom, 15)):
        pairs.append((field.at[:, pl.ds(row, 1)], out.at[pl.ds(0, 4)]))
        pairs.append((remote.at[:, pl.ds(row, 1)], out.at[pl.ds(4, 2)]))
    for copy in transfers(sems, *pairs):
        copy.wait()


def columns_kernel(*refs):
    count = (len(refs) - 3) // 2
    sources, (first, last) = refs[:count], refs[count : count + 2]
    held, sems = refs[count + 2 : -1], refs[-1]
    copies = transfers(sems, *zip(sources, held))
    pick = one_hot((64, 576), lambda i, cell: cell == 32 * (i % 32) + 31 * (i // 32))
    for copy in copies:
        copy.wait()
    low, high = held[-2:]
    start = 0
    for field in held[:-2]:

        @pl.loop(0, field.shape[0])
        def _(t, field=field, start=start):
            block = jnp.concatenate([low[start + t], field[t], high[start + t]], axis=0)
            found = jnp.dot(pick, block.reshape(576, 256), preferred_element_type=F32)
            first[start + t] = found[0:32].astype(BF)
            last[start + t] = found[32:64].astype(BF)

        start += field.shape[0]


def place(taps, groups):
    west_at = one_hot((576, 32), lambda cell, r: cell == 32 * r)
    east_at = one_hot((576, 32), lambda cell, r: cell == 32 * r + 31)

    def put(at, middle, top, bottom, west, east):
        block = jnp.concatenate([top, middle, bottom], axis=0)
        taps[1, at] = block
        block = block.astype(F32)
        column = lax.broadcasted_iota(jnp.int32, block.shape, 1)
        side = jnp.dot(west_at, west, preferred_element_type=F32).reshape(18, 32, 256)
        taps[0, at] = jnp.where(column == 0, side, pltpu.roll(block, 1, 1)).astype(BF)
        side = jnp.dot(east_at, east, preferred_element_type=F32).reshape(18, 32, 256)
        taps[2, at] = jnp.where(column == 31, side, pltpu.roll(block, 31, 1)).astype(BF)

    for first, count, parts in groups:

        @pl.loop(0, count)
        def _(t, first=first, parts=parts):
            put(first + t, *parts(t))


def window(taps, c, frame, b):
    piece = taps[c, frame, pl.ds(b, 16)]
    return piece.reshape(-1, piece.shape[-1])


def weight_terms(taps, slope, half, emit, a):
    lanes = pl.ds(pl.multiple_of(half * 128, 128), 128)
    pieces = [
        taps[c, pl.ds(a, 4), b : b + 16, :, lanes].reshape(2048, 128)
        for b in range(3)
        for c in range(3)
    ]
    value = lax.dot_general(
        jnp.concatenate(pieces, axis=1),
        slope[...].reshape(2048, 256),
        (((0,), (0,)), ((), ())),
        preferred_element_type=F32,
    )
    emit(pl.ds(9 * a, 9), value.reshape(9, 128, 256))


def bias_rows(value):
    high = value.astype(BF).astype(F32)
    return jnp.concatenate([high, value - high, jnp.zeros((112, 256), F32)], axis=0)


def bias_term(slope):
    total = jnp.sum(slope[...].reshape(2048, 256).astype(F32), axis=0, keepdims=True)
    return jnp.broadcast_to(total, (8, 256))


def forward_kernel(*refs):
    sources, bias, outs, held = refs[:9], refs[9], refs[10:15], refs[15:24]
    act, slopes, taps, send, sems = refs[24:]
    copies = transfers(sems, *zip(sources, held))
    field, low, high, left, right, remote, edges, kernel, cotangent = held
    activation, dpre, front, taps_out, send_out = outs
    for copy in copies[:7]:
        copy.wait()
    own = (2, 4, lambda t: (field[t], low[t], high[t], left[t], right[t]))
    far = (
        0,
        2,
        lambda t: (remote[t], edges[t, 0:1], edges[t, 1:2], edges[t, 2], edges[t, 3]),
    )
    place(taps, (own, far))
    taps_copy = pltpu.make_async_copy(taps, taps_out, sems.at[9])
    taps_copy.start()
    for copy in copies[7:]:
        copy.wait()

    @pl.loop(0, 4)
    def _(t):
        total = jnp.broadcast_to(bias[...], (512, 256))
        for a in range(3):
            pieces = [window(taps, c, t + a, b) for b in range(3) for c in range(3)]
            total = total + jnp.dot(
                jnp.concatenate(pieces, axis=1), kernel[a], preferred_element_type=F32
            )
        sig = jax.nn.sigmoid(total)
        act[t] = (total * sig).astype(BF).reshape(16, 32, 256)
        cot = cotangent[t].reshape(512, 256).astype(F32)
        slope = cot * sig * (1.0 + total * (1.0 - sig))
        slopes[t] = slope.astype(BF).reshape(16, 32, 256)

    done = [
        pltpu.make_async_copy(act, activation, sems.at[10]),
        pltpu.make_async_copy(slopes, dpre, sems.at[11]),
        pltpu.make_async_copy(slopes.at[pl.ds(0, 2)], front, sems.at[12]),
    ]
    for copy in done:
        copy.start()

    def emit(at, value):
        send[at] = value.astype(BF)

    @pl.loop(0, 3)
    def _(a):
        weight_terms(taps, slopes, 1 - lax.axis_index("wc"), emit, a)

    send[27] = bias_rows(bias_term(slopes)).astype(BF)
    last = pltpu.make_async_copy(send, send_out, sems.at[13])
    last.start()
    for copy in (taps_copy, *done, last):
        copy.wait()


def weight_kernel(taps_in, dpre_in, own_out, taps, slopes, own, sems):
    pairs = [(dpre_in, slopes), (taps_in.at[:, pl.ds(0, 4)], taps.at[:, pl.ds(0, 4)])]
    pairs += [(taps_in.at[:, pl.ds(f, 1)], taps.at[:, pl.ds(f, 1)]) for f in (4, 5)]
    copies = transfers(sems, *pairs)

    def emit(at, value):
        own[at] = value

    outs = []
    copies[0].wait()
    for a in range(3):
        copies[1 + a].wait()
        weight_terms(taps, slopes, lax.axis_index("wc"), emit, a)
        part = pl.ds(9 * a, 9)
        outs.append(pltpu.make_async_copy(own.at[part], own_out.at[part], sems.at[4 + a]))
        outs[-1].start()
    own[27, 0:8] = bias_term(slopes)
    outs.append(pltpu.make_async_copy(own.at[27, 0:8], own_out.at[27, 0:8], sems.at[7]))
    outs[-1].start()
    for copy in outs:
        copy.wait()


def join_kernel(own_in, received_in, out, own, received, sems):
    copies = transfers(sems, (own_in, own), (received_in, received))
    for copy in copies:
        copy.wait()
    out[0:27] = (own[0:27] + received[0:27].astype(F32)).astype(BF)
    value = own[27, 0:8] + received[27, 0:8].astype(F32) + received[27, 8:16].astype(F32)
    out[27] = bias_rows(value).astype(BF)


def sum_kernel(pieces_in, flag, out, pieces, total, sems):
    copies = transfers(sems, *[(pieces_in.at[i], pieces.at[i]) for i in range(8)])
    for copy in copies:
        copy.wait()

    @pl.loop(0, 7)
    def _(part):
        at = pl.ds(pl.multiple_of(part * 64, 64), 64)
        value = pieces[0, at].astype(F32)
        for i in range(1, 8):
            value = value + pieces[i, at].astype(F32)
        total[at] = value.astype(BF)

    @pl.when(flag[0] == 1)
    def _():
        value = sum(pieces[i, 320:336].astype(F32) for i in range(8))
        total[320:336] = bias_rows(value[0:8] + value[8:16])[0:16].astype(BF)

    copies = transfers(sems, *[(total, out.at[i]) for i in range(8)])
    for copy in copies:
        copy.wait()


def backward_kernel(*refs):
    sources, latent_grad, held = refs[:7], refs[7], refs[8:15]
    grad, taps, sems = refs[15:]
    copies = transfers(sems, *zip(sources, held))
    field, remote, low, high, left, right, kernel = held
    for copy in copies:
        copy.wait()
    own = (0, 4, lambda t: (field[t], low[t], high[t], left[t], right[t]))
    far = (4, 2, lambda t: (remote[t], low[4 + t], high[4 + t], left[4 + t], right[4 + t]))
    place(taps, (own, far))

    @pl.loop(0, 4)
    def _(t):
        total = jnp.zeros((512, 256), F32)
        for a, b, c in itertools.product(range(3), repeat=3):
            total = total + lax.dot_general(
                window(taps, 2 - c, t + 2 - a, 2 - b),
                kernel[9 * a + 3 * b + c],
                (((1,), (1,)), ((), ())),
                preferred_element_type=F32,
            )
        grad[t] = total.astype(BF).reshape(16, 32, 256)

    copy = pltpu.make_async_copy(grad, latent_grad, sems.at[7])
    copy.start()
    copy.wait()


def finish_kernel(scale, turn, half_in, *refs):
    kernel_grad, half, wide, sems = refs[-4 - (turn == 0)], *refs[-3:]
    core = lax.axis_index("wc")
    rows = pl.ds(pl.multiple_of((core if turn == 0 else 1 - core) * 128, 128), 128)
    copies = []
    load = pltpu.make_async_copy(half_in, half, sems.at[9])
    load.start()
    load.wait()
    for k in range(9):
        at = pl.ds(3 * k, 3)
        wide[at] = half[at].astype(F32) * scale
        copies.append(pltpu.make_async_copy(wide.at[at], kernel_grad.at[at, rows], sems.at[k]))
        copies[-1].start()
    if turn == 0:
        bias_grad = refs[1]
        bias_grad[...] = (half[27, 0:1].astype(F32) + half[27, 8:9].astype(F32)) * scale
    for copy in copies:
        copy.wait()


def call(body, outs, n_in, scratch, sems, vmem=24, flops=0, specs=None, out_specs=None, **kwargs):
    return pl.pallas_call(
        body,
        out_shape=outs,
        in_specs=specs or [ANY] * n_in,
        out_specs=out_specs or jax.tree.map(lambda _: ANY, outs),
        scratch_shapes=[*scratch, pltpu.SemaphoreType.DMA((sems,))],
        compiler_params=pltpu.CompilerParams(vmem_limit_bytes=vmem * MIB),
        cost_estimate=pl.CostEstimate(flops=flops, bytes_accessed=4 * MIB, transcendentals=0),
        **kwargs,
    )


def shape(*dims, dtype=BF):
    return jax.ShapeDtypeStruct(dims, dtype)


def buffer(*dims, dtype=BF):
    return pltpu.VMEM(dims, dtype)


def columns_of(low, high, *fields):
    frames = low.shape[0]
    sources = (*fields, low, high)
    return call(
        columns_kernel,
        (shape(frames, 32, 256),) * 2,
        len(sources),
        [buffer(*x.shape) for x in sources],
        len(sources),
        vmem=8,
        out_specs=(VMEM, VMEM),
    )(*sources)


def sum_pieces(pieces, special):
    return call(
        sum_kernel,
        shape(8, 448, 256),
        2,
        [buffer(8, 448, 256), buffer(448, 256)],
        8,
        vmem=8,
        specs=(ANY, pl.BlockSpec(memory_space=pltpu.SMEM)),
    )(pieces, special.astype(jnp.int32).reshape(1))


def finish(scale, turn, half, *base):
    grad = shape(27, 256, 256, dtype=F32)
    outs = (grad, shape(1, 256, dtype=F32)) if turn == 0 else grad
    return call(
        functools.partial(finish_kernel, scale, turn),
        outs,
        1 + turn,
        [buffer(28, 128, 256), buffer(27, 128, 256, dtype=F32)],
        10,
        vmem=8,
        out_specs=(ANY, VMEM) if turn == 0 else ANY,
        input_output_aliases={1: 0} if turn else {},
    )(half, *base)


def shards(latent, kernel, bias, cotangent):
    frames, rows, columns, width = latent.shape
    cells = frames * rows * columns
    for name in AXES:
        cells *= lax.axis_size(name)
    scale = float(1.0 / np.sqrt(np.float32(cells)))
    conv_flops = 2 * 2048 * 27 * 256 * 256
    block, pair, half = (4, 16, 32, 256), (2, 16, 32, 256), (28, 128, 256)
    edge = (4, 1, 32, 256)
    bordered = (3, 6, 18, 32, 256)

    top, bottom, back = call(
        edge_rows_kernel, (shape(*edge), shape(*edge), shape(*pair)), 1, [], 3, vmem=4
    )(latent)
    low = shift(bottom, HA, 1)
    high = shift(top, HA, -1)
    remote = shift(back, "ta", 1)
    first, last = columns_of(low, high, latent)
    left = shift(last, WA, 1)
    right = shift(first, WA, -1)
    edges = jnp.concatenate([low[2:], high[2:], left[2:, None], right[2:, None]], axis=1)
    edges = shift(edges, "ta", 1)

    sources = (latent, low, high, left, right, remote, edges, kernel.reshape(3, 2304, 256))
    sources = (*sources, cotangent)
    activation, dpre, front, taps, send = call(
        forward_kernel,
        (shape(*block), shape(*block), shape(*pair), shape(*bordered), shape(*half)),
        10,
        [buffer(*x.shape) for x in sources]
        + [buffer(*block), buffer(*block), buffer(*bordered), buffer(*half)],
        14,
        vmem=32,
        flops=conv_flops * 3 // 2,
        specs=[ANY] * 9 + [VMEM],
    )(*sources, bias.reshape(1, 256))
    received = lax.ppermute(send, "wc", [(0, 1), (1, 0)])
    remote = shift(front, "ta", -1)
    own = call(
        weight_kernel,
        shape(*half, dtype=F32),
        2,
        [buffer(*bordered), buffer(*block), buffer(*half, dtype=F32)],
        8,
        vmem=24,
        flops=conv_flops // 2,
    )(taps, dpre)
    terms = call(
        join_kernel,
        shape(*half),
        2,
        [buffer(*half, dtype=F32), buffer(*half)],
        2,
        vmem=16,
        out_specs=VMEM,
    )(own, received)

    core = lax.axis_index("wc")
    z = 2 * lax.axis_index("wz") + lax.axis_index("hz")
    spot = [(p - core) % 4 for p in (lax.axis_index("hx"), lax.axis_index("ta"), z)]
    near = sum(w * ((p == 1) | (p == 2)) for w, p in zip((4, 2, 1), spot))
    pieces = exchange(terms.reshape(8, 448, 256), NEAR)
    top, bottom = call(
        more_rows_kernel, (shape(6, 1, 32, 256),) * 2, 2, [], 4, vmem=4
    )(dpre, remote)
    low = shift(bottom, HA, 1)
    high = shift(top, HA, -1)
    first, last = columns_of(low, high, dpre, remote)
    left = shift(last, WA, 1)
    right = shift(first, WA, -1)
    pieces, left, right = lax.optimization_barrier((pieces, left, right))
    pieces = exchange(sum_pieces(pieces, near == 7), FAR)
    sources = (dpre, remote, low, high, left, right, kernel)
    latent_grad = call(
        backward_kernel,
        shape(*block),
        7,
        [buffer(*x.shape) for x in sources] + [buffer(*block), buffer(*bordered)],
        8,
        vmem=32,
        flops=conv_flops,
    )(*sources)
    pieces, latent_grad = lax.optimization_barrier((pieces, latent_grad))
    mine = exchange(sum_pieces(pieces, near == 7), NEAR).reshape(half)
    other = lax.ppermute(mine, "wc", [(0, 1), (1, 0)])
    kernel_grad, bias_grad = finish(scale, 0, mine)
    kernel_grad = finish(scale, 1, other, kernel_grad)
    return (activation, latent_grad, kernel_grad, bias_grad.reshape(256))


def solution(mesh):
    split = Mesh(np.asarray(mesh.devices).reshape(4, 2, 4, 2, 2), AXES)
    placed = P("ta", HA, WA, None)
    return jax.shard_map(
        shards,
        mesh=split,
        in_specs=(placed, P(), P(), placed),
        out_specs=(placed, placed, P(), P()),
        check_vma=False,
    )
```

```python
import functools
import itertools

import jax
import jax.numpy as jnp
import numpy as np
from jax import lax
from jax.experimental import pallas as pl
from jax.experimental.pallas import tpu as pltpu
from jax.sharding import Mesh
from jax.sharding import PartitionSpec as P

AXES = ("ta", "hz", "hx", "wz", "wc")
HA = ("hz", "hx")
WA = ("wz", "wc")
BF = jnp.bfloat16
F32 = jnp.float32
VMEM = pl.BlockSpec(memory_space=pltpu.VMEM)
HBM = pl.BlockSpec(memory_space=pltpu.HBM)
MIB = 1 << 20


def number(x, y, z, core):
    return (((y * 2 + z % 2) * 4 + x) * 2 + z // 2) * 2 + core


def cubes(pairs):
    out = []
    for core in (0, 1):
        for px, py, pz in itertools.product(pairs, repeat=3):
            cube = []
            for a, b, c in itertools.product(range(2), repeat=3):
                place = [(p + core) % 4 for p in (px[a], py[b], pz[c])]
                cube.append(number(*place, core))
            out.append(cube)
    return out


NEAR = cubes(((0, 1), (3, 2)))
FAR = cubes(((0, 3), (1, 2)))


def exchange(pieces, groups):
    return lax.all_to_all(pieces, AXES, 0, 0, axis_index_groups=groups)


def shift(block, axis, distance):
    names = axis if isinstance(axis, tuple) else (axis,)
    count = 1
    for name in names:
        count *= lax.axis_size(name)
    route = [(i, i + distance) for i in range(count) if 0 <= i + distance < count]
    return lax.ppermute(block, axis, route)


def transfers(sems, *pairs):
    copies = [pltpu.make_async_copy(s, d, sems.at[i]) for i, (s, d) in enumerate(pairs)]
    for copy in copies:
        copy.start()
    return copies


def one_hot(shape, hit):
    row = lax.broadcasted_iota(jnp.int32, shape, 0)
    lane = lax.broadcasted_iota(jnp.int32, shape, 1)
    return jnp.where(hit(row, lane), 1.0, 0.0).astype(BF)


def edge_rows_kernel(start, field, top, bottom, frames, sems):
    pairs = [
        (field.at[:, pl.ds(0, 1)], top),
        (field.at[:, pl.ds(15, 1)], bottom),
        (field.at[pl.ds(start, 2)], frames),
    ]
    for copy in transfers(sems, *pairs):
        copy.wait()


def columns_kernel(field, low, high, first, last):
    pick = one_hot((64, 576), lambda i, cell: cell == 32 * (i % 32) + 31 * (i // 32))
    for t in range(4):
        block = jnp.concatenate([low[t], field[t], high[t]], axis=0).reshape(576, 256)
        found = jnp.dot(pick, block, preferred_element_type=F32)
        first[t] = found[0:32].astype(BF)
        last[t] = found[32:64].astype(BF)


def placer(taps):
    west_at = one_hot((576, 32), lambda cell, r: cell == 32 * r)
    east_at = one_hot((576, 32), lambda cell, r: cell == 32 * r + 31)

    def put(at, middle, top, bottom, west, east):
        block = jnp.concatenate([top, middle, bottom], axis=0)
        taps[1, at] = block
        block = block.astype(F32)
        column = lax.broadcasted_iota(jnp.int32, block.shape, 1)
        side = jnp.dot(west_at, west, preferred_element_type=F32).reshape(18, 32, 256)
        taps[0, at] = jnp.where(column == 0, side, pltpu.roll(block, 1, 1)).astype(BF)
        side = jnp.dot(east_at, east, preferred_element_type=F32).reshape(18, 32, 256)
        taps[2, at] = jnp.where(column == 31, side, pltpu.roll(block, 31, 1)).astype(BF)

    return put


def window(taps, c, frame, b):
    piece = taps[c, frame, pl.ds(b, 16)]
    return piece.reshape(-1, piece.shape[-1])


def weight_terms(far, own, slope, half, emit, a):
    lanes = pl.ds(pl.multiple_of(half * 128, 128), 128)

    def block(c, b):
        parts = [own[c, max(a - 2, 0) : a + 2, b : b + 16, :, lanes]]
        if a < 2:
            parts.insert(0, far[c, a:2, b : b + 16, :, lanes])
        return jnp.concatenate(parts, axis=0).reshape(2048, 128)

    value = lax.dot_general(
        jnp.concatenate([block(c, b) for b in range(3) for c in range(3)], axis=1),
        slope[...].reshape(2048, 256),
        (((0,), (0,)), ((), ())),
        preferred_element_type=F32,
    )
    emit(pl.ds(9 * a, 9), value.reshape(9, 128, 256))


def bias_rows(value):
    high = value.astype(BF).astype(F32)
    return jnp.concatenate([high, value - high, jnp.zeros((112, 256), F32)], axis=0)


def bias_term(slope):
    total = jnp.sum(slope[...].reshape(2048, 256).astype(F32), axis=0, keepdims=True)
    return jnp.broadcast_to(total, (8, 256))


def forward(frames, kernel, bias, cot):
    total = jnp.broadcast_to(bias[...], (512, 256))
    for a, (taps, at) in enumerate(frames):
        pieces = [window(taps, c, at, b) for b in range(3) for c in range(3)]
        total = total + jnp.dot(
            jnp.concatenate(pieces, axis=1), kernel[a], preferred_element_type=F32
        )
    sig = jax.nn.sigmoid(total)
    cot = cot.reshape(512, 256).astype(F32)
    slope = cot * sig * (1.0 + total * (1.0 - sig))
    field = (16, 32, 256)
    return (total * sig).astype(BF).reshape(field), slope.astype(BF).reshape(field)


def late_frames_kernel(
    field, low, high, left, right, kernel, cot, bias, activation, slopes, own, act, sems
):
    put = placer(own)

    def put_own(t):
        put(t, field[t], low[t], high[t], left[t], right[t])

    for t in range(3):
        put_own(t)
    for t in range(2):
        act[t], slopes[t] = forward([(own, t + a) for a in range(3)], kernel, bias, cot[t + 2])
        if t == 0:
            put_own(3)
        copy = pltpu.make_async_copy(act.at[t], activation.at[t + 2], sems.at[t])
        copy.start()
    for t in range(2):
        pltpu.make_async_copy(act.at[t], activation.at[t + 2], sems.at[t]).wait()


def early_frames_kernel(*refs):
    remote, edges, own, late, kernel, cot, bias = refs[:7]
    activation, top, bottom, front, slopes, far, act, sems = refs[8:]
    put = placer(far)
    for t in (1, 0):
        put(t, remote[t], edges[t, 0:1], edges[t, 1:2], edges[t, 2], edges[t, 3])
    slopes[2:4] = late[...]
    for t in (1, 0):
        frames = [(far, t + a) if t + a < 2 else (own, t + a - 2) for a in range(3)]
        act[t], slopes[t] = forward(frames, kernel, bias, cot[t])
    pairs = [
        (act, activation.at[pl.ds(0, 2)]),
        (slopes.at[pl.ds(0, 2)], front),
        (slopes.at[:, pl.ds(0, 1)], top),
        (slopes.at[:, pl.ds(15, 1)], bottom),
    ]
    for copy in transfers(sems, *pairs):
        copy.wait()


def weight_kernel(mine, far, own, slopes, out):
    core = lax.axis_index("wc")

    def emit(at, value):
        out[at] = value.astype(out.dtype)

    for a in range(3):
        weight_terms(far, own, slopes, core if mine else 1 - core, emit, a)
    if mine:
        out[27, 0:8] = bias_term(slopes)
    else:
        out[27] = bias_rows(bias_term(slopes)).astype(BF)


def join_kernel(own, received, out):
    out[0:27] = (own[0:27] + received[0:27].astype(F32)).astype(BF)
    value = own[27, 0:8] + received[27, 0:8].astype(F32) + received[27, 8:16].astype(F32)
    out[27] = bias_rows(value).astype(BF)


def sum_kernel(pieces, flag, out, total):
    for part in range(7):
        at = slice(64 * part, 64 * part + 64)
        value = pieces[0, at].astype(F32)
        for i in range(1, 8):
            value = value + pieces[i, at].astype(F32)
        total[at] = value.astype(BF)

    @pl.when(flag[0] == 1)
    def _():
        value = sum(pieces[i, 320:336].astype(F32) for i in range(8))
        total[320:336] = bias_rows(value[0:8] + value[8:16])[0:16].astype(BF)

    for i in range(8):
        out[i] = total[...]


def backward_kernel(
    field, low, high, left, right, remote, edges, kernel, latent_grad, taps
):
    put = placer(taps)

    def put_own(t):
        put(t, field[t], low[t], high[t], left[t], right[t])

    for t in (1, 0):
        put(4 + t, remote[t], edges[t, 0:1], edges[t, 1:2], edges[t, 2], edges[t, 3])
    put_own(3)

    def one(t):
        total = jnp.zeros((512, 256), F32)
        for a, b, c in itertools.product(range(3), repeat=3):
            total = total + lax.dot_general(
                window(taps, 2 - c, t + 2 - a, 2 - b),
                kernel[9 * a + 3 * b + c],
                (((1,), (1,)), ((), ())),
                preferred_element_type=F32,
            )
        latent_grad[t] = total.astype(BF).reshape(16, 32, 256)

    @pl.loop(0, 3)
    def _(i):
        put_own(2 - i)
        one(3 - i)

    one(0)


def finish_kernel(scale, turn, half, *refs):
    kernel_grad, wide, sems = refs[-3 - (turn == 0)], *refs[-2:]
    core = lax.axis_index("wc")
    rows = pl.ds(pl.multiple_of((core if turn == 0 else 1 - core) * 128, 128), 128)
    copies = []
    for k in range(9):
        at = pl.ds(3 * k, 3)
        wide[at] = half[at].astype(F32) * scale
        copies.append(pltpu.make_async_copy(wide.at[at], kernel_grad.at[at, rows], sems.at[k]))
        copies[-1].start()
    if turn == 0:
        bias_grad = refs[1]
        bias_grad[...] = (half[27, 0:1].astype(F32) + half[27, 8:9].astype(F32)) * scale
    for copy in copies:
        copy.wait()


def call(body, outs, n_in, scratch, sems, vmem=24, flops=0, specs=None, out_specs=None, moved=4 << 20, **kwargs):
    return pl.pallas_call(
        body,
        out_shape=outs,
        in_specs=specs or [HBM] * n_in,
        out_specs=out_specs or jax.tree.map(lambda _: HBM, outs),
        scratch_shapes=[*scratch] + [pltpu.SemaphoreType.DMA((sems,))] * (sems > 0),
        compiler_params=pltpu.CompilerParams(vmem_limit_bytes=int(vmem * MIB)),
        cost_estimate=pl.CostEstimate(flops=flops, bytes_accessed=moved, transcendentals=0),
        **kwargs,
    )


def shape(*dims, dtype=BF):
    return jax.ShapeDtypeStruct(dims, dtype)


def buffer(*dims, dtype=BF):
    return pltpu.VMEM(dims, dtype)


def columns_of(*sources):
    outs = (shape(4, 32, 256),) * 2
    return call(columns_kernel, outs, 3, [], 0, vmem=6, moved=1 << 10, specs=[VMEM] * 3, out_specs=(VMEM, VMEM))(*sources)


def edges_of(frames, *parts):
    low, high, left, right = (x[frames] for x in parts)
    return jnp.concatenate([low, high, left[:, None], right[:, None]], axis=1)


def sum_pieces(pieces, special):
    return call(
        sum_kernel,
        shape(8, 448, 256),
        2,
        [buffer(448, 256)],
        0,
        vmem=12,
        specs=(VMEM, pl.BlockSpec(memory_space=pltpu.SMEM)),
        out_specs=VMEM,
    )(pieces, special.astype(jnp.int32).reshape(1))


def finish(scale, turn, half, *base):
    grad = shape(27, 256, 256, dtype=F32)
    outs = (grad, shape(1, 256, dtype=F32)) if turn == 0 else grad
    return call(
        functools.partial(finish_kernel, scale, turn),
        outs,
        1 + turn,
        [buffer(27, 128, 256, dtype=F32)],
        9,
        vmem=8,
        specs=[VMEM] + [HBM] * turn,
        out_specs=(HBM, VMEM) if turn == 0 else HBM,
        input_output_aliases={1: 0} if turn else {},
    )(half, *base)


def shards(latent, kernel, bias, cotangent):
    frames, rows, columns, width = latent.shape
    cells = frames * rows * columns
    for name in AXES:
        cells *= lax.axis_size(name)
    scale = float(1.0 / np.sqrt(np.float32(cells)))
    conv_flops = 2 * 2048 * 27 * 256 * 256
    block, pair, half = (4, 16, 32, 256), (2, 16, 32, 256), (28, 128, 256)
    edge = (4, 1, 32, 256)
    bordered = (3, 6, 18, 32, 256)

    top, bottom, back = call(
        functools.partial(edge_rows_kernel, 2),
        (shape(*edge), shape(*edge), shape(*pair)),
        1,
        [],
        3,
        vmem=4,
    )(latent)
    low = shift(bottom, HA, 1)
    high = shift(top, HA, -1)
    remote = shift(back, "ta", 1)
    first, last = columns_of(latent, low, high)
    left = shift(last, WA, 1)
    right = shift(first, WA, -1)
    edges = shift(edges_of(slice(2, 4), low, high, left, right), "ta", 1)

    grouped, bias = kernel.reshape(3, 2304, 256), bias.reshape(1, 256)
    activation, late, own = call(
        late_frames_kernel,
        (shape(*block), shape(*pair), shape(3, 4, 18, 32, 256)),
        8,
        [buffer(*pair)],
        2,
        vmem=8,
        flops=conv_flops // 2,
        specs=[VMEM] * 8,
        out_specs=(HBM, VMEM, VMEM),
    )(latent, low, high, left, right, grouped, cotangent, bias)
    activation, top, bottom, front, dpre, far = call(
        early_frames_kernel,
        tuple(shape(*x) for x in (block, edge, edge, pair, block, (3, 2, 18, 32, 256))),
        8,
        [buffer(*pair)],
        4,
        vmem=8,
        flops=conv_flops // 2,
        specs=[VMEM] * 7 + [HBM],
        out_specs=(HBM,) * 4 + (VMEM,) * 2,
        input_output_aliases={7: 0},
    )(remote, edges, own, late, grouped, cotangent, bias, activation)
    remote = shift(front, "ta", -1)

    def weight_half(mine):
        return call(
            functools.partial(weight_kernel, mine),
            shape(*half, dtype=F32 if mine else BF),
            3,
            [],
            0,
            vmem=24,
            moved=1 << 10,
            specs=(VMEM, VMEM, VMEM),
            out_specs=VMEM,
        )(far, own, dpre)

    received = lax.ppermute(weight_half(False), "wc", [(0, 1), (1, 0)])
    mine = weight_half(True)
    terms = call(
        join_kernel, shape(*half), 2, [], 0, vmem=16, moved=1 << 10, specs=[VMEM] * 2, out_specs=VMEM
    )(mine, received)

    core = lax.axis_index("wc")
    z = 2 * lax.axis_index("wz") + lax.axis_index("hz")
    spot = [(p - core) % 4 for p in (lax.axis_index("hx"), lax.axis_index("ta"), z)]
    near = sum(w * ((p == 1) | (p == 2)) for w, p in zip((4, 2, 1), spot))
    terms, remote = lax.optimization_barrier((terms, remote))
    pieces = exchange(terms.reshape(8, 448, 256), NEAR)
    low = shift(bottom, HA, 1)
    high = shift(top, HA, -1)
    pieces, low, high = lax.optimization_barrier((pieces, low, high))
    total = sum_pieces(pieces, near == 7)
    first, last = columns_of(dpre, low, high)
    total, first, last = lax.optimization_barrier((total, first, last))
    pieces = exchange(total, FAR)
    left = shift(last, WA, 1)
    right = shift(first, WA, -1)
    edges = shift(edges_of(slice(0, 2), low, high, left, right), "ta", -1)
    pieces, edges = lax.optimization_barrier((pieces, edges))
    total = sum_pieces(pieces, near == 7)
    mine = exchange(total, NEAR).reshape(half)
    sources = (dpre, low, high, left, right, remote, edges, kernel)
    latent_grad = call(
        backward_kernel,
        shape(*block),
        8,
        [buffer(*bordered)],
        0,
        vmem=16,
        flops=conv_flops,
        specs=[VMEM] * 8,
        out_specs=VMEM,
    )(*sources)
    mine, latent_grad = lax.optimization_barrier((mine, latent_grad))
    other = lax.ppermute(mine, "wc", [(0, 1), (1, 0)])
    kernel_grad, bias_grad = finish(scale, 0, mine)
    kernel_grad = finish(scale, 1, other, kernel_grad)
    return (activation, latent_grad, kernel_grad, bias_grad.reshape(256))


def solution(mesh):
    split = Mesh(np.asarray(mesh.devices).reshape(4, 2, 4, 2, 2), AXES)
    placed = P("ta", HA, WA, None)
    return jax.shard_map(
        shards,
        mesh=split,
        in_specs=(placed, P(), P(), placed),
        out_specs=(placed, placed, P(), P()),
        check_vma=False,
    )
```

```python
import functools
import itertools

import jax
import jax.numpy as jnp
import numpy as np
from jax import lax
from jax.experimental import pallas as pl
from jax.experimental.pallas import tpu as pltpu
from jax.sharding import Mesh
from jax.sharding import PartitionSpec as P

AXES = ("ta", "hz", "hx", "wz", "wc")
HA = ("hz", "hx")
WA = ("wz", "wc")
BF = jnp.bfloat16
F32 = jnp.float32
VMEM = pl.BlockSpec(memory_space=pltpu.VMEM)
HBM = pl.BlockSpec(memory_space=pltpu.HBM)
ANY = pl.BlockSpec(memory_space=pl.ANY)
MIB = 1 << 20


def number(x, y, z, core):
    return (((y * 2 + z % 2) * 4 + x) * 2 + z // 2) * 2 + core


def cubes(pairs):
    out = []
    for core in (0, 1):
        for px, py, pz in itertools.product(pairs, repeat=3):
            cube = []
            for a, b, c in itertools.product(range(2), repeat=3):
                place = [(p + core) % 4 for p in (px[a], py[b], pz[c])]
                cube.append(number(*place, core))
            out.append(cube)
    return out


NEAR = cubes(((0, 1), (3, 2)))
FAR = cubes(((0, 3), (1, 2)))


def exchange(pieces, groups):
    return lax.all_to_all(pieces, AXES, 0, 0, axis_index_groups=groups)


def shift(block, axis, distance):
    names = axis if isinstance(axis, tuple) else (axis,)
    count = 1
    for name in names:
        count *= lax.axis_size(name)
    route = [(i, i + distance) for i in range(count) if 0 <= i + distance < count]
    return lax.ppermute(block, axis, route)


def transfers(sems, *pairs):
    copies = [pltpu.make_async_copy(s, d, sems.at[i]) for i, (s, d) in enumerate(pairs)]
    for copy in copies:
        copy.start()
    return copies


def one_hot(shape, hit):
    row = lax.broadcasted_iota(jnp.int32, shape, 0)
    lane = lax.broadcasted_iota(jnp.int32, shape, 1)
    return jnp.where(hit(row, lane), 1.0, 0.0).astype(BF)


def edge_rows_kernel(start, field, top, bottom, frames, sems):
    pairs = [
        (field.at[:, pl.ds(0, 1)], top),
        (field.at[:, pl.ds(15, 1)], bottom),
        (field.at[pl.ds(start, 2)], frames),
    ]
    for copy in transfers(sems, *pairs):
        copy.wait()


def columns_kernel(field, low, high, first, last):
    pick = one_hot((64, 576), lambda i, cell: cell == 32 * (i % 32) + 31 * (i // 32))
    for t in range(4):
        block = jnp.concatenate([low[t], field[t], high[t]], axis=0).reshape(576, 256)
        found = jnp.dot(pick, block, preferred_element_type=F32)
        first[t] = found[0:32].astype(BF)
        last[t] = found[32:64].astype(BF)


def placer(taps):
    west_at = one_hot((576, 32), lambda cell, r: cell == 32 * r)
    east_at = one_hot((576, 32), lambda cell, r: cell == 32 * r + 31)

    def put(at, middle, top, bottom, west, east):
        block = jnp.concatenate([top, middle, bottom], axis=0)
        taps[1, at] = block
        block = block.astype(F32)
        column = lax.broadcasted_iota(jnp.int32, block.shape, 1)
        side = jnp.dot(west_at, west, preferred_element_type=F32).reshape(18, 32, 256)
        taps[0, at] = jnp.where(column == 0, side, pltpu.roll(block, 1, 1)).astype(BF)
        side = jnp.dot(east_at, east, preferred_element_type=F32).reshape(18, 32, 256)
        taps[2, at] = jnp.where(column == 31, side, pltpu.roll(block, 31, 1)).astype(BF)

    return put


def window(taps, c, frame, b):
    piece = taps[c, frame, pl.ds(b, 16)]
    return piece.reshape(-1, piece.shape[-1])


def weight_terms(far, own, slope, half, emit, a):
    lanes = pl.ds(pl.multiple_of(half * 128, 128), 128)

    def block(c, b):
        parts = [own[c, max(a - 2, 0) : a + 2, b : b + 16, :, lanes]]
        if a < 2:
            parts.insert(0, far[c, a:2, b : b + 16, :, lanes])
        return jnp.concatenate(parts, axis=0).reshape(2048, 128)

    value = lax.dot_general(
        jnp.concatenate([block(c, b) for b in range(3) for c in range(3)], axis=1),
        slope[...].reshape(2048, 256),
        (((0,), (0,)), ((), ())),
        preferred_element_type=F32,
    )
    emit(pl.ds(9 * a, 9), value.reshape(9, 128, 256))


def bias_rows(value):
    high = value.astype(BF).astype(F32)
    return jnp.concatenate([high, value - high, jnp.zeros((112, 256), F32)], axis=0)


def bias_term(slope):
    total = jnp.sum(slope[...].reshape(2048, 256).astype(F32), axis=0, keepdims=True)
    return jnp.broadcast_to(total, (8, 256))


def forward(frames, kernel, bias, cot):
    total = jnp.broadcast_to(bias[...], (512, 256))
    for a, (taps, at) in enumerate(frames):
        pieces = [window(taps, c, at, b) for b in range(3) for c in range(3)]
        total = total + jnp.dot(
            jnp.concatenate(pieces, axis=1), kernel[a], preferred_element_type=F32
        )
    sig = jax.nn.sigmoid(total)
    cot = cot.reshape(512, 256).astype(F32)
    slope = cot * sig * (1.0 + total * (1.0 - sig))
    field = (16, 32, 256)
    return (total * sig).astype(BF).reshape(field), slope.astype(BF).reshape(field)


def late_frames_kernel(
    field, low, high, left, right, source, cot, bias, activation, slopes, own, kernel, act, sems
):
    load = pltpu.make_async_copy(source, kernel, sems.at[2])
    load.start()
    put = placer(own)

    def put_own(t):
        put(t, field[t], low[t], high[t], left[t], right[t])

    for t in range(3):
        put_own(t)
    load.wait()
    for t in range(2):
        act[t], slopes[t] = forward([(own, t + a) for a in range(3)], kernel, bias, cot[t + 2])
        if t == 0:
            put_own(3)
        copy = pltpu.make_async_copy(act.at[t], activation.at[t + 2], sems.at[t])
        copy.start()
    for t in range(2):
        pltpu.make_async_copy(act.at[t], activation.at[t + 2], sems.at[t]).wait()


def early_frames_kernel(*refs):
    remote, edges, own, late, kernel, cot, bias = refs[:7]
    activation, top, bottom, front, slopes, far, act, sems = refs[8:]
    put = placer(far)
    for t in (1, 0):
        put(t, remote[t], edges[t, 0:1], edges[t, 1:2], edges[t, 2], edges[t, 3])
    slopes[2:4] = late[...]
    for t in (1, 0):
        frames = [(far, t + a) if t + a < 2 else (own, t + a - 2) for a in range(3)]
        act[t], slopes[t] = forward(frames, kernel, bias, cot[t])
    pairs = [
        (act, activation.at[pl.ds(0, 2)]),
        (slopes.at[pl.ds(0, 2)], front),
        (slopes.at[:, pl.ds(0, 1)], top),
        (slopes.at[:, pl.ds(15, 1)], bottom),
    ]
    for copy in transfers(sems, *pairs):
        copy.wait()


def weight_kernel(mine, far, own, slopes, out):
    core = lax.axis_index("wc")

    def emit(at, value):
        out[at] = value.astype(out.dtype)

    for a in range(3):
        weight_terms(far, own, slopes, core if mine else 1 - core, emit, a)
    if mine:
        out[27, 0:8] = bias_term(slopes)
    else:
        out[27] = bias_rows(bias_term(slopes)).astype(BF)


def join_kernel(own, received, out):
    out[0:27] = (own[0:27] + received[0:27].astype(F32)).astype(BF)
    value = own[27, 0:8] + received[27, 0:8].astype(F32) + received[27, 8:16].astype(F32)
    out[27] = bias_rows(value).astype(BF)


def sum_kernel(pieces, flag, out, total):
    for part in range(7):
        at = slice(64 * part, 64 * part + 64)
        value = pieces[0, at].astype(F32)
        for i in range(1, 8):
            value = value + pieces[i, at].astype(F32)
        total[at] = value.astype(BF)

    @pl.when(flag[0] == 1)
    def _():
        value = sum(pieces[i, 320:336].astype(F32) for i in range(8))
        total[320:336] = bias_rows(value[0:8] + value[8:16])[0:16].astype(BF)

    for i in range(8):
        out[i] = total[...]


def backward_kernel(field, low, high, *refs):
    kernel, latent_grad, taps, held, sems = refs[4], refs[5], refs[6], refs[7:11], refs[11]
    copies = transfers(sems, *zip(refs[:4], held))
    left, right, remote, edges = held
    for copy in copies:
        copy.wait()
    put = placer(taps)

    def put_own(t):
        put(t, field[t], low[t], high[t], left[t], right[t])

    for t in (1, 0):
        put(4 + t, remote[t], edges[t, 0:1], edges[t, 1:2], edges[t, 2], edges[t, 3])
    put_own(3)

    def one(t):
        total = jnp.zeros((512, 256), F32)
        for a, b, c in itertools.product(range(3), repeat=3):
            total = total + lax.dot_general(
                window(taps, 2 - c, t + 2 - a, 2 - b),
                kernel[9 * a + 3 * b + c],
                (((1,), (1,)), ((), ())),
                preferred_element_type=F32,
            )
        latent_grad[t] = total.astype(BF).reshape(16, 32, 256)

    @pl.loop(0, 3)
    def _(i):
        put_own(2 - i)
        one(3 - i)

    one(0)


def finish_kernel(scale, turn, half, *refs):
    kernel_grad, wide, sems = refs[-3 - (turn == 0)], *refs[-2:]
    core = lax.axis_index("wc")
    rows = pl.ds(pl.multiple_of((core if turn == 0 else 1 - core) * 128, 128), 128)
    copies = []
    for k in range(9):
        at = pl.ds(3 * k, 3)
        wide[at] = half[at].astype(F32) * scale
        copies.append(pltpu.make_async_copy(wide.at[at], kernel_grad.at[at, rows], sems.at[k]))
        copies[-1].start()
    if turn == 0:
        bias_grad = refs[1]
        bias_grad[...] = (half[27, 0:1].astype(F32) + half[27, 8:9].astype(F32)) * scale
    for copy in copies:
        copy.wait()


def call(
    body,
    outs,
    n_in,
    scratch,
    sems,
    vmem=24,
    flops=0,
    moved=4 << 20,
    specs=None,
    out_specs=None,
    after=(),
    **kwargs,
):
    specs = list(specs or [HBM] * n_in) + [ANY] * len(after)

    def trimmed(*refs):
        body(*refs[:n_in], *refs[n_in + len(after) :])

    run = pl.pallas_call(
        trimmed,
        out_shape=outs,
        in_specs=specs,
        out_specs=out_specs or jax.tree.map(lambda _: HBM, outs),
        scratch_shapes=[*scratch] + [pltpu.SemaphoreType.DMA((sems,))] * (sems > 0),
        compiler_params=pltpu.CompilerParams(vmem_limit_bytes=int(vmem * MIB)),
        cost_estimate=pl.CostEstimate(flops=flops, bytes_accessed=moved, transcendentals=0),
        **kwargs,
    )
    return lambda *operands: run(*operands, *after)


def shape(*dims, dtype=BF):
    return jax.ShapeDtypeStruct(dims, dtype)


def buffer(*dims, dtype=BF):
    return pltpu.VMEM(dims, dtype)


def columns_of(*sources, after=()):
    return call(
        columns_kernel,
        (shape(4, 32, 256),) * 2,
        3,
        [],
        0,
        vmem=6,
        moved=1 << 10,
        specs=[VMEM] * 3,
        out_specs=(VMEM, VMEM),
        after=after,
    )(*sources)


def in_hbm(x):
    return pltpu.with_memory_space_constraint(x, pltpu.HBM)


def edges_of(frames, *parts):
    low, high, left, right = (x[frames] for x in parts)
    return jnp.concatenate([low, high, left[:, None], right[:, None]], axis=1)


def sum_pieces(pieces, special):
    return call(
        sum_kernel,
        shape(8, 448, 256),
        2,
        [buffer(448, 256)],
        0,
        vmem=12,
        specs=(VMEM, pl.BlockSpec(memory_space=pltpu.SMEM)),
        out_specs=VMEM,
    )(pieces, special.astype(jnp.int32).reshape(1))


def finish(scale, turn, half, *base):
    grad = shape(27, 256, 256, dtype=F32)
    outs = (grad, shape(1, 256, dtype=F32)) if turn == 0 else grad
    return call(
        functools.partial(finish_kernel, scale, turn),
        outs,
        1 + turn,
        [buffer(27, 128, 256, dtype=F32)],
        9,
        vmem=8,
        specs=[VMEM] + [HBM] * turn,
        out_specs=(HBM, VMEM) if turn == 0 else HBM,
        input_output_aliases={1: 0} if turn else {},
    )(half, *base)


def shards(latent, kernel, bias, cotangent):
    frames, rows, columns, width = latent.shape
    cells = frames * rows * columns
    for name in AXES:
        cells *= lax.axis_size(name)
    scale = float(1.0 / np.sqrt(np.float32(cells)))
    conv_flops = 2 * 2048 * 27 * 256 * 256
    block, pair, half = (4, 16, 32, 256), (2, 16, 32, 256), (28, 128, 256)
    edge = (4, 1, 32, 256)
    bordered = (3, 6, 18, 32, 256)

    top, bottom, back = call(
        functools.partial(edge_rows_kernel, 2),
        (shape(*edge), shape(*edge), shape(*pair)),
        1,
        [],
        3,
        vmem=4,
    )(latent)
    low = shift(bottom, HA, 1)
    high = shift(top, HA, -1)
    remote = shift(back, "ta", 1)
    first, last = columns_of(latent, low, high)
    left = shift(last, WA, 1)
    right = shift(first, WA, -1)
    edges = shift(edges_of(slice(2, 4), low, high, left, right), "ta", 1)

    grouped, bias = in_hbm(kernel.reshape(3, 2304, 256)), bias.reshape(1, 256)
    activation, late, own, grouped = call(
        late_frames_kernel,
        (shape(*block), shape(*pair), shape(3, 4, 18, 32, 256), shape(*grouped.shape)),
        8,
        [buffer(*pair)],
        3,
        vmem=8,
        flops=conv_flops // 2,
        specs=[VMEM] * 5 + [HBM] + [VMEM] * 2,
        out_specs=(HBM, VMEM, VMEM, VMEM),
    )(latent, low, high, left, right, grouped, cotangent, bias)
    activation, top, bottom, front, dpre, far = call(
        early_frames_kernel,
        tuple(shape(*x) for x in (block, edge, edge, pair, block, (3, 2, 18, 32, 256))),
        8,
        [buffer(*pair)],
        4,
        vmem=8,
        flops=conv_flops // 2,
        specs=[VMEM] * 7 + [HBM],
        out_specs=(HBM,) * 4 + (VMEM,) * 2,
        input_output_aliases={7: 0},
    )(remote, edges, own, late, grouped, cotangent, bias, activation)
    remote = shift(front, "ta", -1)

    def weight_half(mine):
        return call(
            functools.partial(weight_kernel, mine),
            shape(*half, dtype=F32 if mine else BF),
            3,
            [],
            0,
            vmem=24,
            moved=1 << 10,
            specs=(VMEM, VMEM, VMEM),
            out_specs=VMEM,
        )(far, own, dpre)

    received = lax.ppermute(weight_half(False), "wc", [(0, 1), (1, 0)])
    mine = weight_half(True)
    terms = call(
        join_kernel, shape(*half), 2, [], 0, vmem=16, moved=1 << 10, specs=[VMEM] * 2, out_specs=VMEM
    )(mine, received)

    core = lax.axis_index("wc")
    z = 2 * lax.axis_index("wz") + lax.axis_index("hz")
    spot = [(p - core) % 4 for p in (lax.axis_index("hx"), lax.axis_index("ta"), z)]
    near = sum(w * ((p == 1) | (p == 2)) for w, p in zip((4, 2, 1), spot))
    pieces = exchange(terms.reshape(8, 448, 256), NEAR)
    low = shift(bottom, HA, 1)
    high = shift(top, HA, -1)
    pieces, low, high = lax.optimization_barrier((pieces, low, high))
    total = sum_pieces(pieces, near == 7)
    first, last = columns_of(dpre, low, high, after=(total,))
    total, remote = lax.optimization_barrier((total, remote))
    pieces = exchange(total, FAR)
    left = shift(last, WA, 1)
    right = shift(first, WA, -1)
    edges = shift(edges_of(slice(0, 2), low, high, left, right), "ta", -1)
    pieces, edges = lax.optimization_barrier((pieces, edges))
    total = sum_pieces(pieces, near == 7)
    mine = exchange(total, NEAR).reshape(half)
    sources = (dpre, low, high, left, right, remote, edges, kernel)
    latent_grad = call(
        backward_kernel,
        shape(*block),
        8,
        [buffer(*bordered)] + [buffer(*x.shape) for x in sources[3:7]],
        4,
        vmem=20,
        flops=conv_flops,
        specs=[VMEM] * 3 + [HBM] * 4 + [VMEM],
        out_specs=VMEM,
    )(*sources[:3], *[in_hbm(x) for x in sources[3:7]], kernel)
    mine, latent_grad = lax.optimization_barrier((mine, latent_grad))
    other = lax.ppermute(mine, "wc", [(0, 1), (1, 0)])
    kernel_grad, bias_grad = finish(scale, 0, mine)
    kernel_grad = finish(scale, 1, other, kernel_grad)
    return (activation, latent_grad, kernel_grad, bias_grad.reshape(256))


def solution(mesh):
    split = Mesh(np.asarray(mesh.devices).reshape(4, 2, 4, 2, 2), AXES)
    placed = P("ta", HA, WA, None)
    return jax.shard_map(
        shards,
        mesh=split,
        in_specs=(placed, P(), P(), placed),
        out_specs=(placed, placed, P(), P()),
        check_vma=False,
    )
```

```python
import functools
import itertools

import jax
import jax.numpy as jnp
import numpy as np
from jax import lax
from jax.experimental import pallas as pl
from jax.experimental.pallas import tpu as pltpu
from jax.sharding import Mesh
from jax.sharding import PartitionSpec as P

AXES = ("ta", "hz", "hx", "wz", "wc")
HA = ("hz", "hx")
WA = ("wz", "wc")
BF = jnp.bfloat16
F32 = jnp.float32
VMEM = pl.BlockSpec(memory_space=pltpu.VMEM)
HBM = pl.BlockSpec(memory_space=pltpu.HBM)
ANY = pl.BlockSpec(memory_space=pl.ANY)
MIB = 1 << 20


def number(x, y, z, core):
    return (((y * 2 + z % 2) * 4 + x) * 2 + z // 2) * 2 + core


def cubes(pairs):
    out = []
    for core in (0, 1):
        for px, py, pz in itertools.product(pairs, repeat=3):
            cube = []
            for a, b, c in itertools.product(range(2), repeat=3):
                place = [(p + core) % 4 for p in (px[a], py[b], pz[c])]
                cube.append(number(*place, core))
            out.append(cube)
    return out


NEAR = cubes(((0, 1), (3, 2)))
FAR = cubes(((0, 3), (1, 2)))


def exchange(pieces, groups):
    return lax.all_to_all(pieces, AXES, 0, 0, axis_index_groups=groups)


def shift(block, axis, distance):
    names = axis if isinstance(axis, tuple) else (axis,)
    count = 1
    for name in names:
        count *= lax.axis_size(name)
    route = [(i, i + distance) for i in range(count) if 0 <= i + distance < count]
    return lax.ppermute(block, axis, route)


def transfers(sems, *pairs):
    copies = [pltpu.make_async_copy(s, d, sems.at[i]) for i, (s, d) in enumerate(pairs)]
    for copy in copies:
        copy.start()
    return copies


def one_hot(shape, hit):
    row = lax.broadcasted_iota(jnp.int32, shape, 0)
    lane = lax.broadcasted_iota(jnp.int32, shape, 1)
    return jnp.where(hit(row, lane), 1.0, 0.0).astype(BF)


def edge_rows_kernel(start, field, top, bottom, frames, sems):
    pairs = [
        (field.at[:, pl.ds(0, 1)], top),
        (field.at[:, pl.ds(15, 1)], bottom),
        (field.at[pl.ds(start, 2)], frames),
    ]
    for copy in transfers(sems, *pairs):
        copy.wait()


def columns_kernel(field, low, high, first, last):
    pick = one_hot((64, 576), lambda i, cell: cell == 32 * (i % 32) + 31 * (i // 32))
    for t in range(4):
        block = jnp.concatenate([low[t], field[t], high[t]], axis=0).reshape(576, 256)
        found = jnp.dot(pick, block, preferred_element_type=F32)
        first[t] = found[0:32].astype(BF)
        last[t] = found[32:64].astype(BF)


def placer(taps):
    west_at = one_hot((576, 32), lambda cell, r: cell == 32 * r)
    east_at = one_hot((576, 32), lambda cell, r: cell == 32 * r + 31)

    def put(at, middle, top, bottom, west, east):
        block = jnp.concatenate([top, middle, bottom], axis=0)
        taps[1, at] = block
        block = block.astype(F32)
        column = lax.broadcasted_iota(jnp.int32, block.shape, 1)
        side = jnp.dot(west_at, west, preferred_element_type=F32).reshape(18, 32, 256)
        taps[0, at] = jnp.where(column == 0, side, pltpu.roll(block, 1, 1)).astype(BF)
        side = jnp.dot(east_at, east, preferred_element_type=F32).reshape(18, 32, 256)
        taps[2, at] = jnp.where(column == 31, side, pltpu.roll(block, 31, 1)).astype(BF)

    return put


def window(taps, c, frame, b):
    piece = taps[c, frame, pl.ds(b, 16)]
    return piece.reshape(-1, piece.shape[-1])


def weight_terms(far, own, slope, half, emit, a):
    lanes = pl.ds(pl.multiple_of(half * 128, 128), 128)

    def block(c, b):
        parts = [own[c, max(a - 2, 0) : a + 2, b : b + 16, :, lanes]]
        if a < 2:
            parts.insert(0, far[c, a:2, b : b + 16, :, lanes])
        return jnp.concatenate(parts, axis=0).reshape(2048, 128)

    value = lax.dot_general(
        jnp.concatenate([block(c, b) for b in range(3) for c in range(3)], axis=1),
        slope[...].reshape(2048, 256),
        (((0,), (0,)), ((), ())),
        preferred_element_type=F32,
    )
    emit(pl.ds(9 * a, 9), value.reshape(9, 128, 256))


def bias_rows(value):
    high = value.astype(BF).astype(F32)
    return jnp.concatenate([high, value - high, jnp.zeros((112, 256), F32)], axis=0)


def bias_term(slope):
    total = jnp.sum(slope[...].reshape(2048, 256).astype(F32), axis=0, keepdims=True)
    return jnp.broadcast_to(total, (8, 256))


def forward(frames, kernel, bias, cot):
    total = jnp.broadcast_to(bias[...], (512, 256))
    for a, (taps, at) in enumerate(frames):
        pieces = [window(taps, c, at, b) for b in range(3) for c in range(3)]
        total = total + jnp.dot(
            jnp.concatenate(pieces, axis=1), kernel[a], preferred_element_type=F32
        )
    sig = jax.nn.sigmoid(total)
    cot = cot.reshape(512, 256).astype(F32)
    slope = cot * sig * (1.0 + total * (1.0 - sig))
    field = (16, 32, 256)
    return (total * sig).astype(BF).reshape(field), slope.astype(BF).reshape(field)


def load_kernel(source, held, sems):
    copy = pltpu.make_async_copy(source, held, sems.at[0])
    copy.start()
    copy.wait()


def late_frames_kernel(
    field, low, high, left, right, kernel, cot, bias, activation, slopes, own, act, sems
):
    put = placer(own)

    def put_own(t):
        put(t, field[t], low[t], high[t], left[t], right[t])

    for t in range(3):
        put_own(t)
    for t in range(2):
        act[t], slopes[t] = forward([(own, t + a) for a in range(3)], kernel, bias, cot[t + 2])
        if t == 0:
            put_own(3)
        copy = pltpu.make_async_copy(act.at[t], activation.at[t + 2], sems.at[t])
        copy.start()
    for t in range(2):
        pltpu.make_async_copy(act.at[t], activation.at[t + 2], sems.at[t]).wait()


def early_frames_kernel(*refs):
    remote, edges, own, late, kernel, cot, bias = refs[:7]
    activation, top, bottom, front, slopes, far, act, sems = refs[8:]
    put = placer(far)
    for t in (1, 0):
        put(t, remote[t], edges[t, 0:1], edges[t, 1:2], edges[t, 2], edges[t, 3])
    slopes[2:4] = late[...]
    for t in (1, 0):
        frames = [(far, t + a) if t + a < 2 else (own, t + a - 2) for a in range(3)]
        act[t], slopes[t] = forward(frames, kernel, bias, cot[t])
    pairs = [
        (act, activation.at[pl.ds(0, 2)]),
        (slopes.at[pl.ds(0, 2)], front),
        (slopes.at[:, pl.ds(0, 1)], top),
        (slopes.at[:, pl.ds(15, 1)], bottom),
    ]
    for copy in transfers(sems, *pairs):
        copy.wait()


def weight_kernel(mine, far, own, slopes, out):
    core = lax.axis_index("wc")

    def emit(at, value):
        out[at] = value.astype(out.dtype)

    for a in range(3):
        weight_terms(far, own, slopes, core if mine else 1 - core, emit, a)
    if mine:
        out[27, 0:8] = bias_term(slopes)
    else:
        out[27] = bias_rows(bias_term(slopes)).astype(BF)


def join_kernel(own, received, out):
    out[0:27] = (own[0:27] + received[0:27].astype(F32)).astype(BF)
    value = own[27, 0:8] + received[27, 0:8].astype(F32) + received[27, 8:16].astype(F32)
    out[27] = bias_rows(value).astype(BF)


def sum_kernel(pieces, flag, out, total):
    for part in range(7):
        at = slice(64 * part, 64 * part + 64)
        value = pieces[0, at].astype(F32)
        for i in range(1, 8):
            value = value + pieces[i, at].astype(F32)
        total[at] = value.astype(BF)

    @pl.when(flag[0] == 1)
    def _():
        value = sum(pieces[i, 320:336].astype(F32) for i in range(8))
        total[320:336] = bias_rows(value[0:8] + value[8:16])[0:16].astype(BF)

    for i in range(8):
        out[i] = total[...]


def backward_kernel(field, low, high, *refs):
    kernel, latent_grad, taps, held, sems = refs[4], refs[5], refs[6], refs[7:11], refs[11]
    copies = transfers(sems, *zip(refs[:4], held))
    left, right, remote, edges = held
    for copy in copies:
        copy.wait()
    put = placer(taps)

    def put_own(t):
        put(t, field[t], low[t], high[t], left[t], right[t])

    for t in (1, 0):
        put(4 + t, remote[t], edges[t, 0:1], edges[t, 1:2], edges[t, 2], edges[t, 3])
    put_own(3)

    def one(t):
        total = jnp.zeros((512, 256), F32)
        for a, b, c in itertools.product(range(3), repeat=3):
            total = total + lax.dot_general(
                window(taps, 2 - c, t + 2 - a, 2 - b),
                kernel[9 * a + 3 * b + c],
                (((1,), (1,)), ((), ())),
                preferred_element_type=F32,
            )
        latent_grad[t] = total.astype(BF).reshape(16, 32, 256)

    @pl.loop(0, 3)
    def _(i):
        put_own(2 - i)
        one(3 - i)

    one(0)


def finish_kernel(scale, turn, half, *refs):
    kernel_grad, wide, sems = refs[-3 - (turn == 0)], *refs[-2:]
    core = lax.axis_index("wc")
    rows = pl.ds(pl.multiple_of((core if turn == 0 else 1 - core) * 128, 128), 128)
    copies = []
    for k in range(9):
        at = pl.ds(3 * k, 3)
        wide[at] = half[at].astype(F32) * scale
        copies.append(pltpu.make_async_copy(wide.at[at], kernel_grad.at[at, rows], sems.at[k]))
        copies[-1].start()
    if turn == 0:
        bias_grad = refs[1]
        bias_grad[...] = (half[27, 0:1].astype(F32) + half[27, 8:9].astype(F32)) * scale
    for copy in copies:
        copy.wait()


def call(
    body,
    outs,
    n_in,
    scratch,
    sems,
    vmem=24,
    flops=0,
    moved=4 << 20,
    specs=None,
    out_specs=None,
    after=(),
    **kwargs,
):
    specs = list(specs or [HBM] * n_in) + [ANY] * len(after)

    def trimmed(*refs):
        body(*refs[:n_in], *refs[n_in + len(after) :])

    run = pl.pallas_call(
        trimmed,
        out_shape=outs,
        in_specs=specs,
        out_specs=out_specs or jax.tree.map(lambda _: HBM, outs),
        scratch_shapes=[*scratch] + [pltpu.SemaphoreType.DMA((sems,))] * (sems > 0),
        compiler_params=pltpu.CompilerParams(vmem_limit_bytes=int(vmem * MIB)),
        cost_estimate=pl.CostEstimate(flops=flops, bytes_accessed=moved, transcendentals=0),
        **kwargs,
    )
    return lambda *operands: run(*operands, *after)


def shape(*dims, dtype=BF):
    return jax.ShapeDtypeStruct(dims, dtype)


def buffer(*dims, dtype=BF):
    return pltpu.VMEM(dims, dtype)


def columns_of(*sources, after=()):
    return call(
        columns_kernel,
        (shape(4, 32, 256),) * 2,
        3,
        [],
        0,
        vmem=6,
        moved=1 << 10,
        specs=[VMEM] * 3,
        out_specs=(VMEM, VMEM),
        after=after,
    )(*sources)


def in_hbm(x):
    return pltpu.with_memory_space_constraint(x, pltpu.HBM)


def edges_of(frames, *parts):
    low, high, left, right = (x[frames] for x in parts)
    return jnp.concatenate([low, high, left[:, None], right[:, None]], axis=1)


def sum_pieces(pieces, special):
    return call(
        sum_kernel,
        shape(8, 448, 256),
        2,
        [buffer(448, 256)],
        0,
        vmem=12,
        specs=(VMEM, pl.BlockSpec(memory_space=pltpu.SMEM)),
        out_specs=VMEM,
    )(pieces, special.astype(jnp.int32).reshape(1))


def finish(scale, turn, half, *base):
    grad = shape(27, 256, 256, dtype=F32)
    outs = (grad, shape(1, 256, dtype=F32)) if turn == 0 else grad
    return call(
        functools.partial(finish_kernel, scale, turn),
        outs,
        1 + turn,
        [buffer(27, 128, 256, dtype=F32)],
        9,
        vmem=8,
        specs=[VMEM] + [HBM] * turn,
        out_specs=(HBM, VMEM) if turn == 0 else HBM,
        input_output_aliases={1: 0} if turn else {},
    )(half, *base)


def shards(latent, kernel, bias, cotangent):
    frames, rows, columns, width = latent.shape
    cells = frames * rows * columns
    for name in AXES:
        cells *= lax.axis_size(name)
    scale = float(1.0 / np.sqrt(np.float32(cells)))
    conv_flops = 2 * 2048 * 27 * 256 * 256
    block, pair, half = (4, 16, 32, 256), (2, 16, 32, 256), (28, 128, 256)
    edge = (4, 1, 32, 256)
    bordered = (3, 6, 18, 32, 256)

    top, bottom, back = call(
        functools.partial(edge_rows_kernel, 2),
        (shape(*edge), shape(*edge), shape(*pair)),
        1,
        [],
        3,
        vmem=4,
    )(latent)
    low = shift(bottom, HA, 1)
    high = shift(top, HA, -1)
    remote = shift(back, "ta", 1)
    first, last = columns_of(latent, low, high)
    left = shift(last, WA, 1)
    right = shift(first, WA, -1)
    edges = shift(edges_of(slice(2, 4), low, high, left, right), "ta", 1)

    grouped, bias = in_hbm(kernel.reshape(3, 2304, 256)), bias.reshape(1, 256)
    grouped = call(
        load_kernel, shape(*grouped.shape), 1, [], 1, vmem=4, flops=conv_flops // 4, out_specs=VMEM
    )(grouped)
    activation, late, own = call(
        late_frames_kernel,
        (shape(*block), shape(*pair), shape(3, 4, 18, 32, 256)),
        8,
        [buffer(*pair)],
        2,
        vmem=8,
        flops=conv_flops // 2,
        specs=[VMEM] * 8,
        out_specs=(HBM, VMEM, VMEM),
    )(latent, low, high, left, right, grouped, cotangent, bias)
    activation, top, bottom, front, dpre, far = call(
        early_frames_kernel,
        tuple(shape(*x) for x in (block, edge, edge, pair, block, (3, 2, 18, 32, 256))),
        8,
        [buffer(*pair)],
        4,
        vmem=8,
        flops=conv_flops // 2,
        specs=[VMEM] * 7 + [HBM],
        out_specs=(HBM,) * 4 + (VMEM,) * 2,
        input_output_aliases={7: 0},
    )(remote, edges, own, late, grouped, cotangent, bias, activation)
    remote = shift(front, "ta", -1)

    def weight_half(mine):
        return call(
            functools.partial(weight_kernel, mine),
            shape(*half, dtype=F32 if mine else BF),
            3,
            [],
            0,
            vmem=24,
            moved=1 << 10,
            specs=(VMEM, VMEM, VMEM),
            out_specs=VMEM,
        )(far, own, dpre)

    received = lax.ppermute(weight_half(False), "wc", [(0, 1), (1, 0)])
    mine = weight_half(True)
    terms = call(
        join_kernel, shape(*half), 2, [], 0, vmem=16, moved=1 << 10, specs=[VMEM] * 2, out_specs=VMEM
    )(mine, received)

    core = lax.axis_index("wc")
    z = 2 * lax.axis_index("wz") + lax.axis_index("hz")
    spot = [(p - core) % 4 for p in (lax.axis_index("hx"), lax.axis_index("ta"), z)]
    near = sum(w * ((p == 1) | (p == 2)) for w, p in zip((4, 2, 1), spot))
    pieces = exchange(terms.reshape(8, 448, 256), NEAR)
    low = shift(bottom, HA, 1)
    high = shift(top, HA, -1)
    pieces, low, high = lax.optimization_barrier((pieces, low, high))
    total = sum_pieces(pieces, near == 7)
    first, last = columns_of(dpre, low, high, after=(total,))
    total, remote = lax.optimization_barrier((total, remote))
    pieces = exchange(total, FAR)
    left = shift(last, WA, 1)
    right = shift(first, WA, -1)
    edges = shift(edges_of(slice(0, 2), low, high, left, right), "ta", -1)
    pieces, edges = lax.optimization_barrier((pieces, edges))
    total = sum_pieces(pieces, near == 7)
    mine = exchange(total, NEAR).reshape(half)
    sources = (dpre, low, high, left, right, remote, edges, kernel)
    latent_grad = call(
        backward_kernel,
        shape(*block),
        8,
        [buffer(*bordered)] + [buffer(*x.shape) for x in sources[3:7]],
        4,
        vmem=20,
        flops=conv_flops,
        specs=[VMEM] * 3 + [HBM] * 4 + [VMEM],
        out_specs=VMEM,
    )(*sources[:3], *[in_hbm(x) for x in sources[3:7]], kernel)
    mine, latent_grad = lax.optimization_barrier((mine, latent_grad))
    other = lax.ppermute(mine, "wc", [(0, 1), (1, 0)])
    kernel_grad, bias_grad = finish(scale, 0, mine)
    kernel_grad = finish(scale, 1, other, kernel_grad)
    return (activation, latent_grad, kernel_grad, bias_grad.reshape(256))


def solution(mesh):
    split = Mesh(np.asarray(mesh.devices).reshape(4, 2, 4, 2, 2), AXES)
    placed = P("ta", HA, WA, None)
    return jax.shard_map(
        shards,
        mesh=split,
        in_specs=(placed, P(), P(), placed),
        out_specs=(placed, placed, P(), P()),
        check_vma=False,
    )
```

```python
import functools
import itertools

import jax
import jax.numpy as jnp
import numpy as np
from jax import lax
from jax.experimental import pallas as pl
from jax.experimental.pallas import tpu as pltpu
from jax.sharding import Mesh
from jax.sharding import PartitionSpec as P

AXES = ("ta", "hz", "hx", "wz", "wc")
HA = ("hz", "hx")
WA = ("wz", "wc")
BF = jnp.bfloat16
F32 = jnp.float32
VMEM = pl.BlockSpec(memory_space=pltpu.VMEM)
HBM = pl.BlockSpec(memory_space=pltpu.HBM)
ANY = pl.BlockSpec(memory_space=pl.ANY)
MIB = 1 << 20


def number(x, y, z, core):
    return (((y * 2 + z % 2) * 4 + x) * 2 + z // 2) * 2 + core


def cubes(pairs):
    out = []
    for core in (0, 1):
        for px, py, pz in itertools.product(pairs, repeat=3):
            cube = []
            for a, b, c in itertools.product(range(2), repeat=3):
                place = [(p + core) % 4 for p in (px[a], py[b], pz[c])]
                cube.append(number(*place, core))
            out.append(cube)
    return out


NEAR = cubes(((0, 1), (3, 2)))
FAR = cubes(((0, 3), (1, 2)))


def exchange(pieces, groups):
    return lax.all_to_all(pieces, AXES, 0, 0, axis_index_groups=groups)


def shift(block, axis, distance):
    names = axis if isinstance(axis, tuple) else (axis,)
    count = 1
    for name in names:
        count *= lax.axis_size(name)
    route = [(i, i + distance) for i in range(count) if 0 <= i + distance < count]
    return lax.ppermute(block, axis, route)


def transfers(sems, *pairs):
    copies = [pltpu.make_async_copy(s, d, sems.at[i]) for i, (s, d) in enumerate(pairs)]
    for copy in copies:
        copy.start()
    return copies


def one_hot(shape, hit):
    row = lax.broadcasted_iota(jnp.int32, shape, 0)
    lane = lax.broadcasted_iota(jnp.int32, shape, 1)
    return jnp.where(hit(row, lane), 1.0, 0.0).astype(BF)


def edge_rows_kernel(start, field, top, bottom, frames, sems):
    pairs = [
        (field.at[:, pl.ds(0, 1)], top),
        (field.at[:, pl.ds(15, 1)], bottom),
        (field.at[pl.ds(start, 2)], frames),
    ]
    for copy in transfers(sems, *pairs):
        copy.wait()


def columns_kernel(field, low, high, first, last):
    pick = one_hot((64, 576), lambda i, cell: cell == 32 * (i % 32) + 31 * (i // 32))
    for t in range(4):
        block = jnp.concatenate([low[t], field[t], high[t]], axis=0).reshape(576, 256)
        found = jnp.dot(pick, block, preferred_element_type=F32)
        first[t] = found[0:32].astype(BF)
        last[t] = found[32:64].astype(BF)


def placer(taps):
    west_at = one_hot((576, 32), lambda cell, r: cell == 32 * r)
    east_at = one_hot((576, 32), lambda cell, r: cell == 32 * r + 31)

    def put(at, middle, top, bottom, west, east):
        block = jnp.concatenate([top, middle, bottom], axis=0)
        taps[1, at] = block
        block = block.astype(F32)
        column = lax.broadcasted_iota(jnp.int32, block.shape, 1)
        side = jnp.dot(west_at, west, preferred_element_type=F32).reshape(18, 32, 256)
        taps[0, at] = jnp.where(column == 0, side, pltpu.roll(block, 1, 1)).astype(BF)
        side = jnp.dot(east_at, east, preferred_element_type=F32).reshape(18, 32, 256)
        taps[2, at] = jnp.where(column == 31, side, pltpu.roll(block, 31, 1)).astype(BF)

    return put


def window(taps, c, frame, b):
    piece = taps[c, frame, pl.ds(b, 16)]
    return piece.reshape(-1, piece.shape[-1])


def weight_terms(far, own, slope, half, emit, a):
    lanes = pl.ds(pl.multiple_of(half * 128, 128), 128)

    def block(c, b):
        parts = [own[c, max(a - 2, 0) : a + 2, b : b + 16, :, lanes]]
        if a < 2:
            parts.insert(0, far[c, a:2, b : b + 16, :, lanes])
        return jnp.concatenate(parts, axis=0).reshape(2048, 128)

    value = lax.dot_general(
        jnp.concatenate([block(c, b) for b in range(3) for c in range(3)], axis=1),
        slope[...].reshape(2048, 256),
        (((0,), (0,)), ((), ())),
        preferred_element_type=F32,
    )
    emit(pl.ds(9 * a, 9), value.reshape(9, 128, 256))


def bias_rows(value):
    high = value.astype(BF).astype(F32)
    return jnp.concatenate([high, value - high, jnp.zeros((112, 256), F32)], axis=0)


def bias_term(slope):
    total = jnp.sum(slope[...].reshape(2048, 256).astype(F32), axis=0, keepdims=True)
    return jnp.broadcast_to(total, (8, 256))


def forward(frames, kernel, bias, cot):
    total = jnp.broadcast_to(bias[...], (512, 256))
    for a, (taps, at) in enumerate(frames):
        pieces = [window(taps, c, at, b) for b in range(3) for c in range(3)]
        total = total + jnp.dot(
            jnp.concatenate(pieces, axis=1), kernel[a], preferred_element_type=F32
        )
    sig = jax.nn.sigmoid(total)
    cot = cot.reshape(512, 256).astype(F32)
    slope = cot * sig * (1.0 + total * (1.0 - sig))
    field = (16, 32, 256)
    return (total * sig).astype(BF).reshape(field), slope.astype(BF).reshape(field)


def load_kernel(source, held, sems):
    copy = pltpu.make_async_copy(source, held, sems.at[0])
    copy.start()
    copy.wait()


def late_frames_kernel(
    field, low, high, left, right, kernel, cot, bias, activation, slopes, own, act, sems
):
    put = placer(own)

    def put_own(t):
        put(t, field[t], low[t], high[t], left[t], right[t])

    for t in range(3):
        put_own(t)
    for t in range(2):
        act[t], slopes[t] = forward([(own, t + a) for a in range(3)], kernel, bias, cot[t + 2])
        if t == 0:
            put_own(3)
        copy = pltpu.make_async_copy(act.at[t], activation.at[t + 2], sems.at[t])
        copy.start()
    for t in range(2):
        pltpu.make_async_copy(act.at[t], activation.at[t + 2], sems.at[t]).wait()


def early_frames_kernel(*refs):
    remote, edges, own, late, kernel, cot, bias = refs[:7]
    activation, top, bottom, front, slopes, far, act, sems = refs[8:]
    put = placer(far)
    for t in (1, 0):
        put(t, remote[t], edges[t, 0:1], edges[t, 1:2], edges[t, 2], edges[t, 3])
    slopes[2:4] = late[...]
    for t in (1, 0):
        frames = [(far, t + a) if t + a < 2 else (own, t + a - 2) for a in range(3)]
        act[t], slopes[t] = forward(frames, kernel, bias, cot[t])
    pairs = [
        (act, activation.at[pl.ds(0, 2)]),
        (slopes.at[pl.ds(0, 2)], front),
        (slopes.at[:, pl.ds(0, 1)], top),
        (slopes.at[:, pl.ds(15, 1)], bottom),
    ]
    for copy in transfers(sems, *pairs):
        copy.wait()


def weight_kernel(mine, far, own, slopes, out):
    core = lax.axis_index("wc")

    def emit(at, value):
        out[at] = value.astype(out.dtype)

    for a in range(3):
        weight_terms(far, own, slopes, core if mine else 1 - core, emit, a)
    if mine:
        out[27, 0:8] = bias_term(slopes)
    else:
        out[27] = bias_rows(bias_term(slopes)).astype(BF)


def join_kernel(own, received, out):
    out[0:27] = (own[0:27] + received[0:27].astype(F32)).astype(BF)
    value = own[27, 0:8] + received[27, 0:8].astype(F32) + received[27, 8:16].astype(F32)
    out[27] = bias_rows(value).astype(BF)


def sum_kernel(pieces, flag, out, total):
    for part in range(7):
        at = slice(64 * part, 64 * part + 64)
        value = pieces[0, at].astype(F32)
        for i in range(1, 8):
            value = value + pieces[i, at].astype(F32)
        total[at] = value.astype(BF)

    @pl.when(flag[0] == 1)
    def _():
        value = sum(pieces[i, 320:336].astype(F32) for i in range(8))
        total[320:336] = bias_rows(value[0:8] + value[8:16])[0:16].astype(BF)

    for i in range(8):
        out[i] = total[...]


def backward_kernel(field, low, high, *refs):
    latent_grad, taps, held, sems = refs[5], refs[6], refs[7:12], refs[12]
    copies = transfers(sems, *zip(refs[:5], held))
    left, right, remote, edges, kernel = held
    for copy in copies[:4]:
        copy.wait()
    put = placer(taps)

    def put_own(t):
        put(t, field[t], low[t], high[t], left[t], right[t])

    for t in (1, 0):
        put(4 + t, remote[t], edges[t, 0:1], edges[t, 1:2], edges[t, 2], edges[t, 3])
    put_own(3)
    copies[4].wait()

    def one(t):
        total = jnp.zeros((512, 256), F32)
        for a, b, c in itertools.product(range(3), repeat=3):
            total = total + lax.dot_general(
                window(taps, 2 - c, t + 2 - a, 2 - b),
                kernel[9 * a + 3 * b + c],
                (((1,), (1,)), ((), ())),
                preferred_element_type=F32,
            )
        latent_grad[t] = total.astype(BF).reshape(16, 32, 256)

    @pl.loop(0, 3)
    def _(i):
        put_own(2 - i)
        one(3 - i)

    one(0)


def finish_kernel(scale, turn, half, *refs):
    kernel_grad, wide, sems = refs[-3 - (turn == 0)], *refs[-2:]
    core = lax.axis_index("wc")
    rows = pl.ds(pl.multiple_of((core if turn == 0 else 1 - core) * 128, 128), 128)
    copies = []
    for k in range(9):
        at = pl.ds(3 * k, 3)
        wide[at] = half[at].astype(F32) * scale
        copies.append(pltpu.make_async_copy(wide.at[at], kernel_grad.at[at, rows], sems.at[k]))
        copies[-1].start()
    if turn == 0:
        bias_grad = refs[1]
        bias_grad[...] = (half[27, 0:1].astype(F32) + half[27, 8:9].astype(F32)) * scale
    for copy in copies:
        copy.wait()


def call(
    body,
    outs,
    n_in,
    scratch,
    sems,
    vmem=24,
    flops=0,
    moved=4 << 20,
    specs=None,
    out_specs=None,
    after=(),
    **kwargs,
):
    specs = list(specs or [HBM] * n_in) + [ANY] * len(after)

    def trimmed(*refs):
        body(*refs[:n_in], *refs[n_in + len(after) :])

    run = pl.pallas_call(
        trimmed,
        out_shape=outs,
        in_specs=specs,
        out_specs=out_specs or jax.tree.map(lambda _: HBM, outs),
        scratch_shapes=[*scratch] + [pltpu.SemaphoreType.DMA((sems,))] * (sems > 0),
        compiler_params=pltpu.CompilerParams(vmem_limit_bytes=int(vmem * MIB)),
        cost_estimate=pl.CostEstimate(flops=flops, bytes_accessed=moved, transcendentals=0),
        **kwargs,
    )
    return lambda *operands: run(*operands, *after)


def shape(*dims, dtype=BF):
    return jax.ShapeDtypeStruct(dims, dtype)


def buffer(*dims, dtype=BF):
    return pltpu.VMEM(dims, dtype)


def columns_of(*sources, after=()):
    return call(
        columns_kernel,
        (shape(4, 32, 256),) * 2,
        3,
        [],
        0,
        vmem=6,
        moved=1 << 10,
        specs=[VMEM] * 3,
        out_specs=(VMEM, VMEM),
        after=after,
    )(*sources)


def in_hbm(x):
    return pltpu.with_memory_space_constraint(x, pltpu.HBM)


def edges_of(frames, *parts):
    low, high, left, right = (x[frames] for x in parts)
    return jnp.concatenate([low, high, left[:, None], right[:, None]], axis=1)


def sum_pieces(pieces, special):
    return call(
        sum_kernel,
        shape(8, 448, 256),
        2,
        [buffer(448, 256)],
        0,
        vmem=12,
        specs=(VMEM, pl.BlockSpec(memory_space=pltpu.SMEM)),
        out_specs=VMEM,
    )(pieces, special.astype(jnp.int32).reshape(1))


def finish(scale, turn, half, *base):
    grad = shape(27, 256, 256, dtype=F32)
    outs = (grad, shape(1, 256, dtype=F32)) if turn == 0 else grad
    return call(
        functools.partial(finish_kernel, scale, turn),
        outs,
        1 + turn,
        [buffer(27, 128, 256, dtype=F32)],
        9,
        vmem=8,
        specs=[VMEM] + [HBM] * turn,
        out_specs=(HBM, VMEM) if turn == 0 else HBM,
        input_output_aliases={1: 0} if turn else {},
    )(half, *base)


def shards(latent, kernel, bias, cotangent):
    frames, rows, columns, width = latent.shape
    cells = frames * rows * columns
    for name in AXES:
        cells *= lax.axis_size(name)
    scale = float(1.0 / np.sqrt(np.float32(cells)))
    conv_flops = 2 * 2048 * 27 * 256 * 256
    block, pair, half = (4, 16, 32, 256), (2, 16, 32, 256), (28, 128, 256)
    edge = (4, 1, 32, 256)
    bordered = (3, 6, 18, 32, 256)

    top, bottom, back = call(
        functools.partial(edge_rows_kernel, 2),
        (shape(*edge), shape(*edge), shape(*pair)),
        1,
        [],
        3,
        vmem=4,
    )(latent)
    low = shift(bottom, HA, 1)
    high = shift(top, HA, -1)
    remote = shift(back, "ta", 1)
    first, last = columns_of(latent, low, high)
    left = shift(last, WA, 1)
    right = shift(first, WA, -1)
    edges = shift(edges_of(slice(2, 4), low, high, left, right), "ta", 1)

    grouped, bias = in_hbm(kernel.reshape(3, 2304, 256)), bias.reshape(1, 256)
    grouped = call(
        load_kernel, shape(*grouped.shape), 1, [], 1, vmem=4, flops=conv_flops // 4, out_specs=VMEM
    )(grouped)
    activation, late, own = call(
        late_frames_kernel,
        (shape(*block), shape(*pair), shape(3, 4, 18, 32, 256)),
        8,
        [buffer(*pair)],
        2,
        vmem=8,
        flops=conv_flops // 2,
        specs=[VMEM] * 8,
        out_specs=(HBM, VMEM, VMEM),
    )(latent, low, high, left, right, grouped, cotangent, bias)
    activation, top, bottom, front, dpre, far = call(
        early_frames_kernel,
        tuple(shape(*x) for x in (block, edge, edge, pair, block, (3, 2, 18, 32, 256))),
        8,
        [buffer(*pair)],
        4,
        vmem=8,
        flops=conv_flops // 2,
        specs=[VMEM] * 7 + [HBM],
        out_specs=(HBM,) * 4 + (VMEM,) * 2,
        input_output_aliases={7: 0},
    )(remote, edges, own, late, grouped, cotangent, bias, activation)
    remote = shift(front, "ta", -1)

    def weight_half(mine):
        return call(
            functools.partial(weight_kernel, mine),
            shape(*half, dtype=F32 if mine else BF),
            3,
            [],
            0,
            vmem=24,
            moved=1 << 10,
            specs=(VMEM, VMEM, VMEM),
            out_specs=VMEM,
        )(far, own, dpre)

    received = lax.ppermute(weight_half(False), "wc", [(0, 1), (1, 0)])
    mine = weight_half(True)
    terms = call(
        join_kernel, shape(*half), 2, [], 0, vmem=16, moved=1 << 10, specs=[VMEM] * 2, out_specs=VMEM
    )(mine, received)

    core = lax.axis_index("wc")
    z = 2 * lax.axis_index("wz") + lax.axis_index("hz")
    spot = [(p - core) % 4 for p in (lax.axis_index("hx"), lax.axis_index("ta"), z)]
    near = sum(w * ((p == 1) | (p == 2)) for w, p in zip((4, 2, 1), spot))
    pieces = exchange(terms.reshape(8, 448, 256), NEAR)
    low = shift(bottom, HA, 1)
    high = shift(top, HA, -1)
    pieces, low, high = lax.optimization_barrier((pieces, low, high))
    total = sum_pieces(pieces, near == 7)
    first, last = columns_of(dpre, low, high, after=(total,))
    total, remote = lax.optimization_barrier((total, remote))
    pieces = exchange(total, FAR)
    left = shift(last, WA, 1)
    right = shift(first, WA, -1)
    edges = shift(edges_of(slice(0, 2), low, high, left, right), "ta", -1)
    pieces, edges = lax.optimization_barrier((pieces, edges))
    total = sum_pieces(pieces, near == 7)
    mine = exchange(total, NEAR).reshape(half)
    sources = (dpre, low, high, left, right, remote, edges, kernel)
    latent_grad = call(
        backward_kernel,
        shape(*block),
        8,
        [buffer(*bordered)] + [buffer(*x.shape) for x in sources[3:8]],
        5,
        vmem=20,
        flops=conv_flops,
        specs=[VMEM] * 3 + [HBM] * 5,
        out_specs=VMEM,
    )(*sources[:3], *[in_hbm(x) for x in sources[3:8]])
    mine, latent_grad = lax.optimization_barrier((mine, latent_grad))
    other = lax.ppermute(mine, "wc", [(0, 1), (1, 0)])
    kernel_grad, bias_grad = finish(scale, 0, mine)
    kernel_grad = finish(scale, 1, other, kernel_grad)
    return (activation, latent_grad, kernel_grad, bias_grad.reshape(256))


def solution(mesh):
    split = Mesh(np.asarray(mesh.devices).reshape(4, 2, 4, 2, 2), AXES)
    placed = P("ta", HA, WA, None)
    return jax.shard_map(
        shards,
        mesh=split,
        in_specs=(placed, P(), P(), placed),
        out_specs=(placed, placed, P(), P()),
        check_vma=False,
    )
```
